32 devices in a mesh: groups: 2 (over y), gx: 4 (over z), gy: 2 (over x), gz: 2 (over core).
Axes of the slice: x: 2, y: 2, z: 4, core: 2. Of those that a mesh axis runs over, the one named last changes fastest.
Arguments:
- atoms: bfloat16 [8, 2, 8, 16, 128], P(('groups', 'gx'), 'gy', 'gz'), parts along dimension 0, may hold values from -6 to 6
- places: bfloat16 [8, 2, 8, 3, 16], P(('groups', 'gx'), 'gy', 'gz'), parts along dimension 0, may hold values from 0 to 1
- counts: int32 [8, 2, 8], P(('groups', 'gx'), 'gy', 'gz'), parts along dimension 0, may hold values from 8 to 16, as said below
- in_weight: bfloat16 [128, 128], replicated, may hold values from -0.5 to 0.5
- basis_weight: bfloat16 [50, 128], replicated, may hold values from -0.875 to 0.875
- basis_bias: float32 [128], replicated, may hold values from -3 to 3
- filter_weight: bfloat16 [128, 128], replicated, may hold values from -0.5 to 0.5
- filter_bias: float32 [128], replicated, may hold values from -3 to 3
- dense_weight: bfloat16 [128, 128], replicated, may hold values from -0.5 to 0.5
- dense_bias: float32 [128], replicated, may hold values from -3 to 3
- final_weight: bfloat16 [128, 128], replicated, may hold values from -0.5 to 0.5
- final_bias: float32 [128], replicated, may hold values from -3 to 3
Outputs:
- updated: bfloat16 [8, 2, 8, 16, 128], P(('groups', 'gx'), 'gy', 'gz'), parts along dimension 0
The draws below stay inside these ranges and needn't reach their ends.
There are 2 independent parts, one for each index of `groups`. The reference program is written for one: setup_inputs(seed, part) draws one part's arguments, and reference() takes and returns one part's arrays. A program takes and returns all parts, laid end to end along the dimension named above; an argument that names none is the same for every part. Nothing has to cross between parts.
Inputs may be any that keep to these rules, and one draw needn't show every extreme that they name: Each cell's atoms fill its first counts slots; some cell holds 16 atoms in every draw.
All inputs are finite; a program needn't handle non-finite values.
Results may differ from the reference program's by a relative error of at most 0.008.
Values may be sent and summed in bfloat16 or wider, within the bound.
No kernel may reach another device: no remote copies, remote signals or barrier semaphores. Data moves between devices by JAX's collectives and lax.ppermute only.
A program may use at most 64 MiB of HBM per device.

```python
import math
import jax
import jax.numpy as jnp
import numpy as np
from jax import lax

F = 128
K = 50
A = 16
NX = 4
NY = 2
NZ = 8


def draw_counts(key, part):
    drawn = jax.random.randint(key, (NX, NY, NZ), A // 2, A + 1)
    return drawn.at[0, 0, 0].set(A).astype(jnp.int32)


def levels(own_key, extent, split, low, high):
    def one(dim, blocks):
        heights = jax.random.uniform(jax.random.fold_in(jax.random.fold_in(own_key, 6), dim), (blocks,), jnp.float32, low / len(split), high / len(split))
        return jnp.repeat(jnp.exp(heights), extent[dim] // blocks).reshape((-1,) + (1,) * (len(extent) - dim - 1))

    level = one(*split[0])
    for cut in split[1:]:
        level = level * one(*cut)
    return level


def noise(rng, dims, scale, most, cuts=(), held_as=jnp.bfloat16):
    values = scale * jax.random.normal(rng, dims, jnp.float32)
    if cuts:
        values = values * levels(rng, dims, cuts, -0.22, 0.18)
    return jnp.clip(values, -most, most).astype(held_as)


def setup_inputs(seed: int = 0, part: int = 0) -> dict:
    keys = jax.random.split(jax.random.key(seed), 13)
    part_splits = jax.random.split(jax.random.fold_in(keys[12], part), 13)
    atoms = noise(part_splits[0], (NX, NY, NZ, A, F), 1.0, 6.0, ((0, 4), (1, 2), (2, 2)))
    places = jnp.clip(1.0 * jax.random.uniform(part_splits[1], (NX, NY, NZ, 3, A), jnp.float32) ** levels(part_splits[1], (NX, NY, NZ, 3, A), ((0, 4), (1, 2), (2, 2)), -0.2, 0.2), 0.0, 1.0).astype(jnp.bfloat16)
    counts = draw_counts(jax.random.fold_in(jax.random.fold_in(keys[12], part), 71), part)
    in_weight = noise(keys[3], (F, F), F ** -0.5, 0.5)
    basis_weight = noise(keys[4], (K, F), K ** -0.5, 0.875)
    basis_bias = noise(keys[5], (F,), 0.5, 3.0, (), jnp.float32)
    filter_weight = noise(keys[6], (F, F), F ** -0.5, 0.5)
    filter_bias = noise(keys[7], (F,), 0.5, 3.0, (), jnp.float32)
    dense_weight = noise(keys[8], (F, F), F ** -0.5, 0.5)
    dense_bias = noise(keys[9], (F,), 0.5, 3.0, (), jnp.float32)
    final_weight = noise(keys[10], (F, F), F ** -0.5, 0.5)
    final_bias = noise(keys[11], (F,), 0.5, 3.0, (), jnp.float32)
    return {"atoms": atoms, "places": places, "counts": counts, "in_weight": in_weight, "basis_weight": basis_weight, "basis_bias": basis_bias, "filter_weight": filter_weight, "filter_bias": filter_bias, "dense_weight": dense_weight, "dense_bias": dense_bias, "final_weight": final_weight, "final_bias": final_bias}


CELL_EDGE = 5.0
BASIS_GAMMA = 10.0
LOG_TWO = 0.6931471805599453

def shifted_softplus(values):
    return jax.nn.softplus(values) - LOG_TWO

def neighbour_offsets():
    return np.array([[p, q, r] for p in (-1, 0, 1) for q in (-1, 0, 1) for r in (-1, 0, 1)], np.int32)

def pair_filters(coords_i, occupied_i, coords_j, occupied_j, offset, itself, basis_weight, basis_bias, filter_weight, filter_bias):
    n = coords_i.shape[0]
    a = coords_i.shape[2]
    k = basis_weight.shape[0]
    f = basis_weight.shape[1]
    separation = coords_j[:, :, None, :] + offset[None, :, None, None] - coords_i[:, :, :, None]
    radius = CELL_EDGE * jnp.sqrt(lax.optimization_barrier(jnp.sum(separation * separation, axis=1)))
    diagonal = jnp.eye(a, dtype=jnp.float32)
    allowed = occupied_i[:, :, None] * occupied_j[:, None, :] * (1.0 - itself * diagonal)[None]
    inside = jnp.where(radius < CELL_EDGE, 0.5 * (jnp.cos(jnp.pi * radius / CELL_EDGE) + 1.0), 0.0)
    weight = (allowed * inside).reshape(1, n * a * a)
    centers = lax.iota(jnp.float32, k) * (CELL_EDGE / (k - 1))
    distance_gap = radius.reshape(1, n * a * a) - centers[:, None]
    expand = jnp.exp(-BASIS_GAMMA * distance_gap * distance_gap).astype(jnp.bfloat16)
    hidden = jnp.dot(basis_weight.T, expand, preferred_element_type=jnp.float32) + basis_bias[:, None]
    hidden = shifted_softplus(hidden).astype(jnp.bfloat16)
    filters = jnp.dot(filter_weight.T, hidden, preferred_element_type=jnp.float32) + filter_bias[:, None]
    return (filters * weight).astype(jnp.bfloat16).reshape(f, n, a, a)

def reference(atoms, places, counts, in_weight, basis_weight, basis_bias, filter_weight, filter_bias, dense_weight, dense_bias, final_weight, final_bias):
    grid_x, grid_y, grid_z, a, f = atoms.shape
    cell_count = grid_x * grid_y * grid_z
    cell_block = math.gcd(cell_count, 16)
    blocks = cell_count // cell_block
    projected = jnp.dot(atoms.reshape(-1, f), in_weight, preferred_element_type=jnp.float32).astype(jnp.bfloat16).reshape(atoms.shape)
    coords = places.astype(jnp.float32)
    occupied = (lax.iota(jnp.int32, a)[None, None, None, :] < counts[:, :, :, None]).astype(jnp.float32)

    def per_offset(summed, offset):
        moves = (-offset[0], -offset[1], -offset[2])
        coords_near = jnp.roll(coords, moves, axis=(0, 1, 2))
        occupied_near = jnp.roll(occupied, moves, axis=(0, 1, 2))
        projected_near = jnp.roll(projected, moves, axis=(0, 1, 2))
        itself = (jnp.sum(jnp.abs(offset)) == 0).astype(jnp.float32)
        along = offset.astype(jnp.float32)

        def per_block(pieces):
            coords_i, occupied_i, coords_j, occupied_j, features_j = pieces
            filters = pair_filters(coords_i, occupied_i, coords_j, occupied_j, along, itself, basis_weight, basis_bias, filter_weight, filter_bias)
            return jnp.einsum('fnij,njf->nif', filters.astype(jnp.float32), features_j.astype(jnp.float32))
        pieces = (coords.reshape(blocks, cell_block, 3, a), occupied.reshape(blocks, cell_block, a), coords_near.reshape(blocks, cell_block, 3, a), occupied_near.reshape(blocks, cell_block, a), projected_near.reshape(blocks, cell_block, a, f))
        message = lax.map(per_block, pieces).reshape(grid_x, grid_y, grid_z, a, f)
        return (summed + message, None)
    summed, _ = lax.scan(per_offset, jnp.zeros((grid_x, grid_y, grid_z, a, f), jnp.float32), jnp.asarray(neighbour_offsets()))
    message = summed.astype(jnp.bfloat16).reshape(-1, f)
    inner = shifted_softplus(jnp.dot(message, dense_weight, preferred_element_type=jnp.float32) + dense_bias).astype(jnp.bfloat16)
    update = jnp.dot(inner, final_weight, preferred_element_type=jnp.float32) + final_bias
    result = (atoms.reshape(-1, f).astype(jnp.float32) + update) * occupied.reshape(-1, 1)
    return result.astype(jnp.bfloat16).reshape(atoms.shape)
```

```python
import math

import jax
import jax.numpy as jnp
import numpy as np
from jax import lax
from jax.experimental import pallas as pl
from jax.experimental.pallas import tpu as pltpu
from jax.sharding import PartitionSpec as P

LOG_TWO = 0.6931471805599453
BASIS_GAMMA = 10.0
CELL_EDGE = 5.0
FAR = 8.0
PAD_K = 64

COS_SERIES = [(-1.0) ** m * (math.pi / 2) ** (2 * m) / math.factorial(2 * m) for m in range(9)]


def ssp(values):
    return jnp.log(0.5 + jnp.exp(values - LOG_TWO))


def pack_kernel(counts_ref, atoms_ref, places_ref, out_ref):
    cells, a, f = atoms_ref.shape
    for c in range(cells):
        out_ref[c * a : (c + 1) * a, :] = atoms_ref[c]
    slot = lax.broadcasted_iota(jnp.int32, (3, a), 1)
    out_ref[cells * a :, :] = jnp.zeros((out_ref.shape[0] - cells * a, f), out_ref.dtype)
    spots = [
        jnp.where(slot < counts_ref[c], places_ref[c].astype(jnp.float32), FAR)
        for c in range(cells)
    ]
    table = jnp.stack(spots, axis=1).reshape(3 * cells, a)
    out_ref[cells * a : cells * a + 3 * cells, :a] = table.astype(out_ref.dtype)


def split_bf16(values, parts):
    out = []
    rest = values
    for _ in range(parts):
        head = rest.astype(jnp.bfloat16)
        out.append(head)
        rest = rest - head.astype(jnp.float32)
    return out


def main_kernel(layout, counts_ref, *refs):
    cells, a, f, k, y_count, block_of = layout
    n_blocks = len(block_of["names"])
    blocks = refs[:n_blocks]
    (in_w, basis_w, basis_b, filt_w, filt_b, dense_w, dense_b, final_w, final_b, out_ref) = refs[
        n_blocks : n_blocks + 10
    ]
    proj, zrow, rads, wgts, acc, w1_ref, w2_ref = refs[n_blocks + 10 :]
    wide = cells + 2
    lanes = a * a
    f32, bf16 = jnp.float32, jnp.bfloat16

    w1_ref[...] = jnp.zeros(w1_ref.shape, bf16)
    w1_ref[:, :k] = basis_w[...].astype(f32).T.astype(bf16)
    bias = (basis_b[...] - LOG_TWO).T
    for n, part in enumerate(split_bf16(bias, 3)):
        w1_ref[:, PAD_K + n : PAD_K + n + 1] = part
    w2_ref[...] = jnp.zeros(w2_ref.shape, bf16)
    w2_ref[:, :f] = filt_w[...].astype(f32).T.astype(bf16)
    for n, part in enumerate(split_bf16(filt_b[...].T, 2)):
        w2_ref[:, f + n : f + n + 1] = part

    def place_of(x, y, z):
        if z < 0:
            return blocks[block_of[(y, -1)]], x, cells - 1
        if z >= cells:
            return blocks[block_of[(y, 1)]], x, 0
        return blocks[block_of[(y, 0)]], x, z

    reps = 128 // a
    for x in range(3):
        for y in range(y_count):
            for z in range(-1, cells + 1):
                ref, bx, bz = place_of(x, y, z)
                rows = ref[bx, bz * a : (bz + 1) * a, :]
                rows = jnp.concatenate([rows] * reps, axis=0)
                tile = lax.dot_general(
                    in_w[...], rows, (((0,), (1,)), ((), ())), preferred_element_type=f32
                )
                proj[(x * y_count + y) * wide + z + 1] = tile.astype(bf16).astype(f32)

    row_id = lax.broadcasted_iota(jnp.int32, (f, lanes), 0)
    lane_id = lax.broadcasted_iota(jnp.int32, (f, lanes), 1)
    by_j = (row_id == lane_id % a).astype(f32).astype(bf16)
    by_i = (row_id == lane_id // a).astype(f32).astype(bf16)
    base = cells * a
    for x in range(3):
        for y in range(y_count):
            tables = {}
            for side in (-1, 0, 1):
                b = block_of[(y, side)]
                if b not in tables:
                    tables[b] = jnp.dot(
                        blocks[b][x, base : base + 16, :], by_j, preferred_element_type=f32
                    )
            for d in range(3):
                at = ((x * y_count + y) * 3) + d
                low = tables[block_of[(y, -1)]][d * cells + cells - 1 : d * cells + cells]
                mid = tables[block_of[(y, 0)]][d * cells : (d + 1) * cells]
                high = tables[block_of[(y, 1)]][d * cells : d * cells + 1]
                zrow[at, 0:1, :] = low
                zrow[at, 1 : 1 + cells, :] = mid
                zrow[at, 1 + cells : 2 + cells, :] = high
    own = jnp.dot(
        blocks[block_of[(0, 0)]][1, base : base + 16, :], by_i, preferred_element_type=f32
    )
    own = [own[d * cells : (d + 1) * cells] for d in range(3)]
    small = lax.broadcasted_iota(jnp.int32, (cells, lanes), 1)
    other = small % a != small // a
    for p in range(3):
        for q in range(3):
            y = block_of["y_index"][q]
            for r in range(3):
                shift = (p - 1, q - 1, r - 1)
                square = jnp.zeros((cells, lanes), f32)
                for d in range(3):
                    there = zrow[(p * y_count + y) * 3 + d, r : r + cells, :]
                    gap = there + float(shift[d]) - own[d]
                    square = square + gap * gap
                radius = CELL_EDGE * jnp.sqrt(square)
                cosine = jnp.full(square.shape, COS_SERIES[-1], f32)
                for term in COS_SERIES[-2::-1]:
                    cosine = cosine * square + term
                keep = radius < CELL_EDGE
                if shift == (0, 0, 0):
                    keep = keep & other
                at = (p * 3 + q) * 3 + r
                rads[at] = radius
                wgts[at] = jnp.where(keep, cosine * cosine, 0.0)

    acc[...] = jnp.zeros(acc.shape, f32)
    centers = lax.broadcasted_iota(jnp.int32, (PAD_K, 128), 0).astype(f32) * (CELL_EDGE / (k - 1))
    centers = jnp.concatenate([centers] * (lanes // 128), axis=1)
    ones = jnp.ones((16, lanes), bf16)

    def step(t, carry):
        p = t // 3
        q = t - p * 3
        y = jnp.where(q == 1, 0, 1) if y_count == 2 else (q + 2) % 3
        first = (p * y_count + y) * wide
        for c in range(cells):
            total = None
            for r in range(3):
                radius = rads[t * 3 + r, c : c + 1, :]
                gap = radius - centers
                grid = jnp.exp(gap * gap * (-BASIS_GAMMA)).astype(bf16)
                hidden = jnp.dot(
                    w1_ref[...], jnp.concatenate([grid, ones], axis=0), preferred_element_type=f32
                )
                hidden = jnp.log(0.5 + jnp.exp(hidden)).astype(bf16)
                weight = wgts[t * 3 + r, c : c + 1, :]
                weight = jnp.broadcast_to(weight, (16, lanes)).astype(bf16)
                hidden = (hidden.reshape(f // 16, 16, lanes) * weight[None]).reshape(f, lanes)
                filt = jnp.dot(
                    w2_ref[...], jnp.concatenate([hidden, weight], axis=0), preferred_element_type=f32
                )
                feat = proj[first + c + r]
                term = filt * jnp.concatenate([feat] * (lanes // 128), axis=1)
                total = term if total is None else total + term
            acc[c] += total
        return carry

    lax.fori_loop(0, 9, step, 0)

    rows = lax.broadcasted_iota(jnp.int32, (a, lanes), 0)
    cols = lax.broadcasted_iota(jnp.int32, (a, lanes), 1)
    pick = (rows == cols // a).astype(f32).astype(bf16)
    messages = []
    for c in range(cells):
        head, tail = split_bf16(acc[c], 2)
        dims = (((1,), (1,)), ((), ()))
        messages.append(
            lax.dot_general(pick, head, dims, preferred_element_type=f32)
            + lax.dot_general(pick, tail, dims, preferred_element_type=f32)
        )
    message = jnp.concatenate(messages, axis=0).astype(bf16)
    inner = jnp.dot(message, dense_w[...], preferred_element_type=f32) + dense_b[...]
    inner = (jax.nn.softplus(inner) - LOG_TWO).astype(bf16)
    update = jnp.dot(inner, final_w[...], preferred_element_type=f32) + final_b[...]
    slot = lax.broadcasted_iota(jnp.int32, (a, f), 0)
    own_block = blocks[block_of[(0, 0)]]
    for c in range(cells):
        here = own_block[1, c * a : (c + 1) * a, :].astype(f32)
        value = here + update[c * a : (c + 1) * a]
        out_ref[c] = jnp.where(slot < counts_ref[c], value, 0.0).astype(bf16)


def shifted(value, steps):
    axes = [axis for axis, s in steps if s % lax.axis_size(axis)]
    if not axes:
        return value
    sizes = [lax.axis_size(axis) for axis in axes]
    moves = [dict(steps)[axis] for axis in axes]
    pairs = []
    for at in np.ndindex(*sizes):
        to = [(i + s) % n for i, s, n in zip(at, moves, sizes)]
        pairs.append((int(np.ravel_multi_index(at, sizes)), int(np.ravel_multi_index(to, sizes))))
    return lax.ppermute(value, tuple(axes), pairs)


def shards(
    atoms,
    places,
    counts,
    in_weight,
    basis_weight,
    basis_bias,
    filter_weight,
    filter_bias,
    dense_weight,
    dense_bias,
    final_weight,
    final_bias,
):
    cells_x, cells_y, cells_z, a, f = atoms.shape
    assert cells_x == 1 and cells_y == 1
    cells = cells_z
    k = basis_weight.shape[0]
    vmem = pl.BlockSpec(memory_space=pltpu.VMEM)
    smem = pl.BlockSpec(memory_space=pltpu.SMEM)
    counts = counts.reshape(cells)
    packed = pl.pallas_call(
        pack_kernel,
        out_shape=jax.ShapeDtypeStruct((cells * a + 16, f), jnp.bfloat16),
        in_specs=[smem, vmem, vmem],
        out_specs=vmem,
    )(counts, atoms.reshape(cells, a, f), places.reshape(cells, 3, a))
    below = shifted(packed, [("gx", 1)])
    above = shifted(packed, [("gx", -1)])
    line = jnp.stack([below, packed, above])

    y_size, z_size = lax.axis_size("gy"), lax.axis_size("gz")
    y_steps = [0] if y_size == 1 else [0, 1] if y_size == 2 else [0, 1, -1]
    y_index = [0, 0, 0] if y_size == 1 else [1, 0, 1] if y_size == 2 else [2, 0, 1]
    names, block_of = [], {"names": None, "y_index": y_index}
    for yi, y in enumerate(y_steps):
        for z in (0, -1, 1):
            name = (y % y_size, z % z_size)
            if name not in names:
                names.append(name)
            block_of[(yi, z)] = names.index(name)
    block_of["names"] = names
    blocks = [shifted(line, [("gy", -y), ("gz", -z)]) for y, z in names]

    y_count = len(y_steps)
    lanes = a * a
    layout = (cells, a, f, k, y_count, block_of)
    halo = 3 * y_count * (cells + 2)
    out = pl.pallas_call(
        lambda *refs: main_kernel(layout, *refs),
        out_shape=jax.ShapeDtypeStruct((cells, a, f), jnp.bfloat16),
        in_specs=[smem] + [vmem] * (len(blocks) + 9),
        out_specs=vmem,
        scratch_shapes=[
            pltpu.VMEM((halo, f, 128), jnp.float32),
            pltpu.VMEM((3 * y_count * 3, 8, lanes), jnp.float32),
            pltpu.VMEM((27, cells, lanes), jnp.float32),
            pltpu.VMEM((27, cells, lanes), jnp.float32),
            pltpu.VMEM((cells, f, lanes), jnp.float32),
            pltpu.VMEM((f, PAD_K + 16), jnp.bfloat16),
            pltpu.VMEM((f, f + 16), jnp.bfloat16),
        ],
    )(
        counts,
        *blocks,
        in_weight,
        basis_weight,
        basis_bias.reshape(1, f),
        filter_weight,
        filter_bias.reshape(1, f),
        dense_weight,
        dense_bias.reshape(1, f),
        final_weight,
        final_bias.reshape(1, f),
    )
    return out.reshape(atoms.shape)


def solution(mesh):
    placed = (
        P(("groups", "gx"), "gy", "gz", None, None),
        P(("groups", "gx"), "gy", "gz", None, None),
        P(("groups", "gx"), "gy", "gz"),
    ) + (P(),) * 9
    return jax.shard_map(
        shards,
        mesh=mesh,
        in_specs=placed,
        out_specs=P(("groups", "gx"), "gy", "gz", None, None),
        check_vma=False,
    )
```

```python
import math

import jax
import jax.numpy as jnp
import numpy as np
from jax import lax
from jax.experimental import pallas as pl
from jax.experimental.pallas import tpu as pltpu
from jax.sharding import PartitionSpec as P

LOG_TWO = 0.6931471805599453
LOG2_E = 1.4426950408889634
BASIS_GAMMA = 10.0
CELL_EDGE = 5.0
GAP_SCALE = math.sqrt(BASIS_GAMMA * LOG2_E)
FAR = 8.0
PAD_K = 64
EXTRA = 16

COS_SERIES = [(-1.0) ** m * (math.pi / 2) ** (2 * m) / math.factorial(2 * m) for m in range(9)]
F32, BF16 = jnp.float32, jnp.bfloat16
NT = (((1,), (1,)), ((), ()))


def split_bf16(values, parts):
    out = []
    rest = values
    for _ in range(parts):
        head = rest.astype(BF16)
        out.append(head)
        rest = rest - head.astype(F32)
    return out


def pack_kernel(counts_ref, atoms_ref, places_ref, out_ref):
    cells, a, f = atoms_ref.shape
    for c in range(cells):
        out_ref[c * a : (c + 1) * a, :] = atoms_ref[c]
    cell = lax.broadcasted_iota(jnp.int32, (cells, a), 0)
    slot = lax.broadcasted_iota(jnp.int32, (cells, a), 1)
    filled = jnp.zeros((cells, a), jnp.int32)
    for c in range(cells):
        filled = jnp.where(cell == c, counts_ref[c], filled)
    out_ref[cells * a :, :] = jnp.zeros((out_ref.shape[0] - cells * a, f), BF16)
    spots = [jnp.where(slot < filled, places_ref[d].astype(F32), FAR) for d in range(3)]
    table = jnp.concatenate(spots, axis=0)
    out_ref[cells * a : cells * a + 3 * cells, :a] = table.astype(BF16)


def spread(a, lanes, rows, by_j):
    row = lax.broadcasted_iota(jnp.int32, (rows, lanes), 0)
    lane = lax.broadcasted_iota(jnp.int32, (rows, lanes), 1)
    return (row == (lane % a if by_j else lane // a)).astype(F32).astype(BF16)


def project(rows, in_w, reps):
    return lax.dot_general(
        in_w[...], jnp.concatenate([rows] * reps, axis=0), (((0,), (1,)), ((), ())), preferred_element_type=F32
    )


def pair_terms(there, own, moves, drop):
    square = None
    for d, move in enumerate(moves):
        gap = there[d] - own[d]
        if len(move) == 2:
            gap = jnp.minimum(jnp.abs(gap + 1.0), jnp.abs(gap - 1.0))
        else:
            gap = gap + float(move[0])
        square = gap * gap if square is None else square + gap * gap
    far = jnp.sqrt(square)
    cosine = jnp.full(square.shape, COS_SERIES[-1], F32)
    for term in COS_SERIES[-2::-1]:
        cosine = cosine * square + term
    keep = CELL_EDGE * far < CELL_EDGE
    if drop is not None:
        keep = keep & drop
    return far * (CELL_EDGE * GAP_SCALE), jnp.where(keep, cosine * cosine * LOG_TWO, 0.0)


def add_pairs(units, cells, lanes, w1, w2, acc, k, f):
    reps = lanes // 128
    centers = lax.broadcasted_iota(jnp.int32, (PAD_K, 128), 0).astype(F32)
    centers = centers * (GAP_SCALE * CELL_EDGE / (k - 1))
    centers = jnp.concatenate([centers] * reps, axis=1)
    ones = jnp.ones((EXTRA, lanes), BF16)
    totals = [None] * cells
    left = [sum(u[0] == c for u in units) for c in range(cells)]
    first, second = {}, {}
    for n in range(len(units) + 2):
        if n < len(units):
            gap = (units[n][1]() - centers).astype(BF16)
            grid = jnp.exp2(gap * -gap)
            first[n] = jnp.dot(w1[...], jnp.concatenate([grid, ones], axis=0), preferred_element_type=F32)
        if 0 <= n - 1 < len(units):
            hidden = first.pop(n - 1).astype(BF16)
            hidden = jnp.log2(jnp.exp2(hidden) + jnp.array(0.5, BF16))
            weight = jnp.broadcast_to(units[n - 1][2](), (EXTRA, lanes)).astype(BF16)
            hidden = (hidden.reshape(f // EXTRA, EXTRA, lanes) * weight[None]).reshape(f, lanes)
            second[n - 1] = jnp.dot(w2[...], jnp.concatenate([hidden, weight], axis=0), preferred_element_type=F32)
        if 0 <= n - 2 < len(units):
            c = units[n - 2][0]
            term = second.pop(n - 2) * jnp.concatenate([units[n - 2][3]()] * reps, axis=1)
            totals[c] = term if totals[c] is None else totals[c] + term
            left[c] -= 1
            if left[c] == 0:
                acc[c] += totals[c]


def near_kernel(
    sizes, line, in_w, basis_w, basis_b, filt_w, filt_b, acc, w1, w2, proj, zrow, rads, wgts
):
    cells, a, f, k = sizes
    lanes = a * a
    w1[...] = jnp.zeros(w1.shape, BF16)
    w1[:, :k] = (basis_w[...].astype(F32).T * LOG2_E).astype(BF16)
    bias = (basis_b[...] * LOG2_E - 1.0).T
    for n, part in enumerate(split_bf16(bias, 3)):
        w1[:, PAD_K + n : PAD_K + n + 1] = part
    w2[...] = jnp.zeros(w2.shape, BF16)
    w2[:, :f] = filt_w[...].astype(F32).T.astype(BF16)
    for n, part in enumerate(split_bf16(filt_b[...].T * LOG2_E, 2)):
        w2[:, f + n : f + n + 1] = part
    base = cells * a
    by_j, by_i = spread(a, lanes, f, True), spread(a, lanes, f, False)
    own = jnp.dot(line[1, base : base + 16, :], by_i, preferred_element_type=F32)
    own = [own[d * cells : (d + 1) * cells] for d in range(3)]
    small = lax.broadcasted_iota(jnp.int32, (cells, lanes), 1)
    other = small % a != small // a
    for p in range(3):
        for c in range(cells):
            proj[p * cells + c] = project(line[p, c * a : (c + 1) * a, :], in_w, 128 // a)
        table = jnp.dot(line[p, base : base + 16, :], by_j, preferred_element_type=F32)
        for d in range(3):
            mid = table[d * cells : (d + 1) * cells]
            zrow[d, 0:cells, :] = mid
            zrow[d, 2 : 2 + cells, :] = mid
            zrow[d, 1 : 1 + cells, :] = mid
        for r in range(3):
            there = [zrow[d, r : r + cells, :] for d in range(3)]
            moves = ((1 - p,), (0,), (r - 1,))
            rads[p * 3 + r], wgts[p * 3 + r] = pair_terms(there, own, moves, other if p == 1 and r == 1 else None)
    acc[...] = jnp.zeros(acc.shape, F32)

    def step(p, carry):
        units = []
        for c in range(cells):
            for r in range(3):
                if 0 <= c + r - 1 < cells:
                    units.append((
                        c,
                        lambda c=c, r=r: rads[p * 3 + r, c : c + 1, :],
                        lambda c=c, r=r: wgts[p * 3 + r, c : c + 1, :],
                        lambda c=c, r=r: proj[p * cells + c + r - 1],
                    ))
        add_pairs(units, cells, lanes, w1, w2, acc, k, f)
        return carry

    lax.fori_loop(0, 3, step, 0)


def far_kernel(sizes, plan, counts_ref, *refs):
    cells, a, f, k = sizes
    block_of, ways, n_blocks = plan
    blocks, refs = refs[:n_blocks], refs[n_blocks:]
    near, w1, w2, in_w, dense_w, dense_b, final_w, final_b, out_ref, acc, proj, zrow, rads, wgts = refs
    lanes, wide, n_ways = a * a, cells + 2, len(ways)
    base = cells * a
    by_j, by_i = spread(a, lanes, f, True), spread(a, lanes, f, False)
    own_block = blocks[block_of[(0, 0)]]
    own = jnp.dot(own_block[1, base : base + 16, :], by_i, preferred_element_type=F32)
    own = [own[d * cells : (d + 1) * cells] for d in range(3)]

    def place_of(way, z):
        if z < 0:
            return blocks[block_of[(way, -1)]], cells - 1
        if z >= cells:
            return blocks[block_of[(way, 1)]], 0
        return blocks[block_of[(way, 0)]], z

    for p in range(3):
        for way in range(n_ways):
            at = p * n_ways + way
            for z in range(-1, cells + 1):
                if way == 0 and 0 <= z < cells:
                    continue
                ref, here = place_of(way, z)
                proj[at * wide + z + 1] = project(ref[p, here * a : (here + 1) * a, :], in_w, 128 // a)
            tables = {}
            for side in (-1, 0, 1):
                b = block_of[(way, side)]
                if b not in tables:
                    tables[b] = jnp.dot(blocks[b][p, base : base + 16, :], by_j, preferred_element_type=F32)
            for d in range(3):
                low, mid, high = (tables[block_of[(way, side)]] for side in (-1, 0, 1))
                zrow[d, 0:1, :] = low[d * cells + cells - 1 : d * cells + cells]
                zrow[d, 1 : 1 + cells, :] = mid[d * cells : (d + 1) * cells]
                zrow[d, 1 + cells : wide, :] = high[d * cells : d * cells + 1]
            for r in range(3):
                if way == 0 and r == 1:
                    continue
                there = [zrow[d, r : r + cells, :] for d in range(3)]
                moves = ((1 - p,), ways[way], (r - 1,))
                rads[at * 3 + r], wgts[at * 3 + r] = pair_terms(there, own, moves, None)
    acc[...] = jnp.zeros(acc.shape, F32)

    def step(p, carry):
        units = []
        for c in range(cells):
            for way in range(n_ways):
                for r in range(3):
                    if way == 0 and 0 <= c + r - 1 < cells:
                        continue
                    at = p * n_ways + way
                    units.append((
                        c,
                        lambda at=at, c=c, r=r: rads[at * 3 + r, c : c + 1, :],
                        lambda at=at, c=c, r=r: wgts[at * 3 + r, c : c + 1, :],
                        lambda at=at, c=c, r=r: proj[at * wide + c + r],
                    ))
        add_pairs(units, cells, lanes, w1, w2, acc, k, f)
        return carry

    lax.fori_loop(0, 3, step, 0)

    pick = spread(a, lanes, a, False)
    messages = []
    for c in range(cells):
        head, tail = split_bf16(acc[c] + near[c], 2)
        messages.append(
            lax.dot_general(pick, head, NT, preferred_element_type=F32)
            + lax.dot_general(pick, tail, NT, preferred_element_type=F32)
        )
    message = jnp.concatenate(messages, axis=0).astype(BF16)
    inner = jnp.dot(message, dense_w[...], preferred_element_type=F32) + dense_b[...]
    inner = (jax.nn.softplus(inner) - LOG_TWO).astype(BF16)
    update = jnp.dot(inner, final_w[...], preferred_element_type=F32) + final_b[...]
    slot = lax.broadcasted_iota(jnp.int32, (a, f), 0)
    for c in range(cells):
        here = own_block[1, c * a : (c + 1) * a, :].astype(F32)
        value = here + update[c * a : (c + 1) * a]
        out_ref[c] = jnp.where(slot < counts_ref[c], value, 0.0).astype(BF16)


def shifted(value, steps):
    axes = [axis for axis, s in steps if s % lax.axis_size(axis)]
    if not axes:
        return value
    sizes = [lax.axis_size(axis) for axis in axes]
    moves = [dict(steps)[axis] for axis in axes]
    pairs = []
    for at in np.ndindex(*sizes):
        to = [(i + s) % n for i, s, n in zip(at, moves, sizes)]
        pairs.append((int(np.ravel_multi_index(at, sizes)), int(np.ravel_multi_index(to, sizes))))
    return lax.ppermute(value, tuple(axes), pairs)


def on_chip(value):
    return pltpu.with_memory_space_constraint(value, pltpu.VMEM)


def shards(
    atoms,
    places,
    counts,
    in_weight,
    basis_weight,
    basis_bias,
    filter_weight,
    filter_bias,
    dense_weight,
    dense_bias,
    final_weight,
    final_bias,
):
    cells_x, cells_y, cells_z, a, f = atoms.shape
    assert cells_x == 1 and cells_y == 1
    cells = cells_z
    k = basis_weight.shape[0]
    lanes = a * a
    sizes = (cells, a, f, k)
    vmem = pl.BlockSpec(memory_space=pltpu.VMEM)
    smem = pl.BlockSpec(memory_space=pltpu.SMEM)
    counts = counts.reshape(cells)
    packed = pl.pallas_call(
        pack_kernel,
        out_shape=pltpu.VMEM((cells * a + 16, f), BF16),
        in_specs=[smem, vmem, vmem],
        out_specs=vmem,
    )(counts, atoms.reshape(cells, a, f), jnp.swapaxes(places, 2, 3).reshape(3, cells, a))
    above = shifted(packed, [("gx", -1)])
    below = shifted(packed, [("gx", 1)])
    line = jnp.stack([above, packed, below])

    y_size, z_size = lax.axis_size("gy"), lax.axis_size("gz")
    y_steps, ways = ([0, 1], [(0,), (1, -1)]) if y_size == 2 else ([0, 1, -1], [(0,), (1,), (-1,)])
    names, block_of = [], {}
    for way, y in enumerate(y_steps):
        for z in (0, -1, 1):
            name = (y % y_size, z % z_size)
            if name not in names:
                names.append(name)
            block_of[(way, z)] = names.index(name)
    blocks = [shifted(line, [("gy", -y), ("gz", -z)]) for y, z in names]

    n_ways = len(ways)
    terms = [pltpu.VMEM((9 * n_ways, cells, lanes), F32)] * 2
    near, w1, w2 = pl.pallas_call(
        lambda *refs: near_kernel(sizes, *refs),
        out_shape=[
            pltpu.VMEM((cells, f, lanes), F32),
            pltpu.VMEM((f, PAD_K + EXTRA), BF16),
            pltpu.VMEM((f, f + EXTRA), BF16),
        ],
        in_specs=[vmem] * 6,
        out_specs=[vmem] * 3,
        scratch_shapes=[pltpu.VMEM((3 * cells, f, 128), F32), pltpu.VMEM((3, 8, lanes), F32)]
        + [pltpu.VMEM((9, cells, lanes), F32)] * 2,
        cost_estimate=pl.CostEstimate(flops=10**9, transcendentals=10**6, bytes_accessed=10**6),
    )(
        *map(
            on_chip,
            (line, in_weight, basis_weight, basis_bias.reshape(1, f), filter_weight, filter_bias.reshape(1, f)),
        )
    )
    out = pl.pallas_call(
        lambda *refs: far_kernel(sizes, (block_of, ways, len(blocks)), *refs),
        out_shape=jax.ShapeDtypeStruct((cells, a, f), BF16),
        in_specs=[smem] + [vmem] * (len(blocks) + 8),
        out_specs=vmem,
        scratch_shapes=[
            pltpu.VMEM((cells, f, lanes), F32),
            pltpu.VMEM((3 * n_ways * (cells + 2), f, 128), F32),
            pltpu.VMEM((3, 8, lanes), F32),
        ]
        + terms,
        cost_estimate=pl.CostEstimate(flops=10**9, transcendentals=10**6, bytes_accessed=10**6),
    )(
        counts,
        *map(
            on_chip,
            (
                *blocks,
                near,
                w1,
                w2,
                in_weight,
                dense_weight,
                dense_bias.reshape(1, f),
                final_weight,
                final_bias.reshape(1, f),
            ),
        ),
    )
    return out.reshape(atoms.shape)


def solution(mesh):
    placed = (
        P(("groups", "gx"), "gy", "gz", None, None),
        P(("groups", "gx"), "gy", "gz", None, None),
        P(("groups", "gx"), "gy", "gz"),
    ) + (P(),) * 9
    return jax.shard_map(
        shards,
        mesh=mesh,
        in_specs=placed,
        out_specs=P(("groups", "gx"), "gy", "gz", None, None),
        check_vma=False,
    )
```

```python
import math

import jax
import jax.numpy as jnp
import numpy as np
from jax import lax
from jax.experimental import pallas as pl
from jax.experimental.pallas import tpu as pltpu
from jax.sharding import PartitionSpec as P

LOG_TWO = 0.6931471805599453
LOG2_E = 1.4426950408889634
BASIS_GAMMA = 10.0
CELL_EDGE = 5.0
GAP_SCALE = math.sqrt(BASIS_GAMMA * LOG2_E)
FAR = 8.0
PAD_K = 64
EXTRA = 16

COS_SERIES = [(-1.0) ** m * (math.pi / 2) ** (2 * m) / math.factorial(2 * m) for m in range(9)]
F32, BF16 = jnp.float32, jnp.bfloat16
NT = (((1,), (1,)), ((), ()))


def split_bf16(values, parts):
    out = []
    rest = values
    for _ in range(parts):
        head = rest.astype(BF16)
        out.append(head)
        rest = rest - head.astype(F32)
    return out


def pack_kernel(counts_ref, atoms_ref, places_ref, out_ref):
    cells, a, f = atoms_ref.shape
    for c in range(cells):
        out_ref[c * a : (c + 1) * a, :] = atoms_ref[c]
    cell = lax.broadcasted_iota(jnp.int32, (cells, a), 0)
    slot = lax.broadcasted_iota(jnp.int32, (cells, a), 1)
    filled = jnp.zeros((cells, a), jnp.int32)
    for c in range(cells):
        filled = jnp.where(cell == c, counts_ref[c], filled)
    out_ref[cells * a :, :] = jnp.zeros((out_ref.shape[0] - cells * a, f), BF16)
    spots = [jnp.where(slot < filled, places_ref[d].astype(F32), FAR) for d in range(3)]
    table = jnp.concatenate(spots, axis=0)
    out_ref[cells * a : cells * a + 3 * cells, :a] = table.astype(BF16)


def spread(a, lanes, rows, by_j):
    row = lax.broadcasted_iota(jnp.int32, (rows, lanes), 0)
    lane = lax.broadcasted_iota(jnp.int32, (1, lanes), 1)
    return (row == (lane % a if by_j else lane // a)).astype(F32).astype(BF16)


def project(block, p, c, a, in_t):
    rows = block[p, c * a : (c + 1) * a, :]
    return lax.dot_general(in_t[...], jnp.concatenate([rows] * (128 // a), axis=0), NT, preferred_element_type=F32)


def spots(block, p, base, by_j):
    return jnp.dot(block[p, base : base + 16, :], by_j[...], preferred_element_type=F32)


def pair_terms(there, own, moves, drop):
    square = None
    for d, move in enumerate(moves):
        gap = there[d] - own[d]
        if len(move) == 2:
            gap = jnp.minimum(jnp.abs(gap + 1.0), jnp.abs(gap - 1.0))
        else:
            gap = gap + float(move[0])
        square = gap * gap if square is None else square + gap * gap
    far = jnp.sqrt(square)
    cosine = jnp.full(square.shape, COS_SERIES[-1], F32)
    for term in COS_SERIES[-2::-1]:
        cosine = cosine * square + term
    keep = CELL_EDGE * far < CELL_EDGE
    if drop is not None:
        keep = keep & drop
    return far * (CELL_EDGE * GAP_SCALE), jnp.where(keep, cosine * cosine * LOG_TWO, 0.0)


def add_pairs(units, cells, lanes, w1, w2, acc, k, f):
    reps = lanes // 128
    centers = lax.broadcasted_iota(jnp.int32, (PAD_K, 128), 0).astype(F32)
    centers = centers * (GAP_SCALE * CELL_EDGE / (k - 1))
    centers = jnp.concatenate([centers] * reps, axis=1)
    ones = jnp.ones((EXTRA, lanes), BF16)
    totals = [None] * cells
    left = [sum(u[0] == c for u in units) for c in range(cells)]
    first, second = {}, {}
    for n in range(len(units) + 2):
        if n < len(units):
            gap = (units[n][1]() - centers).astype(BF16)
            grid = jnp.exp2(gap * -gap)
            first[n] = jnp.dot(w1[...], jnp.concatenate([grid, ones], axis=0), preferred_element_type=F32)
        if 0 <= n - 1 < len(units):
            hidden = first.pop(n - 1).astype(BF16)
            hidden = jnp.log2(jnp.exp2(hidden) + jnp.array(0.5, BF16))
            weight = jnp.broadcast_to(units[n - 1][2](), (EXTRA, lanes)).astype(BF16)
            hidden = (hidden.reshape(f // EXTRA, EXTRA, lanes) * weight[None]).reshape(f, lanes)
            second[n - 1] = jnp.dot(w2[...], jnp.concatenate([hidden, weight], axis=0), preferred_element_type=F32)
        if 0 <= n - 2 < len(units):
            c = units[n - 2][0]
            term = second.pop(n - 2) * jnp.concatenate([units[n - 2][3]()] * reps, axis=1)
            totals[c] = term if totals[c] is None else totals[c] + term
            left[c] -= 1
            if left[c] == 0:
                acc[c] += totals[c]


def unit(rads, wgts, proj, c, at, cell):
    return (c, lambda: rads[at, c : c + 1, :], lambda: wgts[at, c : c + 1, :], lambda: proj[cell])


def inside(cells):
    return [(c, r) for c in range(cells) for r in range(3) if 0 <= c + r - 1 < cells]


def window(zrow, tables, cells):
    for d in range(3):
        low, mid, high = (t[d * cells : (d + 1) * cells] for t in tables)
        zrow[d, 1 + cells : 1 + 2 * cells, :] = high
        zrow[d, 1 : 1 + cells, :] = mid
        zrow[d, 0:1, :] = low[cells - 1 : cells]


def own_rows(own, cells):
    return [own[d * cells : (d + 1) * cells, :] for d in range(3)]


def first_kernel(
    sizes, packed, in_w, basis_w, basis_b, filt_w, filt_b, dense_w, dense_b, final_w, final_b,
    acc, w1, w2, in_t, dense_o, final_o, biases, by_j, pick, own, proj, zrow, rads, wgts
):
    cells, a, f, k = sizes
    lanes, base = a * a, cells * a
    w1[...] = jnp.zeros(w1.shape, BF16)
    w1[:, :k] = (basis_w[...].astype(F32).T * LOG2_E).astype(BF16)
    bias = (basis_b[...] * LOG2_E - 1.0).T
    for n, part in enumerate(split_bf16(bias, 3)):
        w1[:, PAD_K + n : PAD_K + n + 1] = part
    w2[...] = jnp.zeros(w2.shape, BF16)
    w2[:, :f] = filt_w[...].astype(F32).T.astype(BF16)
    for n, part in enumerate(split_bf16(filt_b[...].T * LOG2_E, 2)):
        w2[:, f + n : f + n + 1] = part
    in_t[...] = in_w[...].astype(F32).T.astype(BF16)
    dense_o[...] = dense_w[...]
    final_o[...] = final_w[...]
    biases[0:1, :] = dense_b[...]
    biases[1:2, :] = final_b[...]
    by_j[...] = spread(a, lanes, f, True)
    pick[...] = spread(a, lanes, a, False)
    line = packed.reshape(1, *packed.shape)
    own[...] = spots(line, 0, base, spread(a, lanes, f, False))
    table = spots(line, 0, base, by_j)
    window(zrow, (table, table, table), cells)
    small = lax.broadcasted_iota(jnp.int32, (1, lanes), 1)
    other = small % a != small // a
    for c in range(cells):
        proj[c] = project(line, 0, c, a, in_t)
    for r in range(3):
        there = [zrow[d, r : r + cells, :] for d in range(3)]
        moves = ((0,), (0,), (r - 1,))
        rads[r], wgts[r] = pair_terms(there, own_rows(own, cells), moves, other if r == 1 else None)
    acc[...] = jnp.zeros(acc.shape, F32)
    units = [unit(rads, wgts, proj, c, r, c + r - 1) for c, r in inside(cells)]
    add_pairs(units, cells, lanes, w1, w2, acc, k, f)


def near_kernel(sizes, line, low_line, high_line, own, w1, w2, in_t, by_j, acc, proj, zrow, rads, wgts):
    cells, a, f, k = sizes
    lanes, base, wide = a * a, cells * a, cells + 2
    for p in range(3):
        proj[p * wide] = project(low_line, p, cells - 1, a, in_t)
        proj[p * wide + cells + 1] = project(high_line, p, 0, a, in_t)
        for c in range(cells if p != 1 else 0):
            proj[p * wide + c + 1] = project(line, p, c, a, in_t)
        window(zrow, [spots(l, p, base, by_j) for l in (low_line, line, high_line)], cells)
        for r in range(3):
            there = [zrow[d, r : r + cells, :] for d in range(3)]
            moves = ((1 - p,), (0,), (r - 1,))
            rads[p * 3 + r], wgts[p * 3 + r] = pair_terms(there, own_rows(own, cells), moves, None)
    acc[...] = jnp.zeros(acc.shape, F32)

    def step(t, carry):
        p = 2 * t
        units = [unit(rads, wgts, proj, c, p * 3 + r, p * wide + c + r) for c in range(cells) for r in range(3)]
        add_pairs(units, cells, lanes, w1, w2, acc, k, f)
        return carry

    lax.fori_loop(0, 2, step, 0)
    units = [unit(rads, wgts, proj, c, 3 + r, wide + c + r) for c, r in ((0, 0), (cells - 1, 2))]
    add_pairs(units, cells, lanes, w1, w2, acc, k, f)


def plane_kernel(sizes, ways, *refs):
    cells, a, f, k = sizes
    lines, refs = refs[: len(ways)], refs[len(ways) :]
    own, w1, w2, in_t, by_j, acc, proj, zrow, rads, wgts = refs
    lanes, base, n_ways = a * a, cells * a, len(ways)
    for p in range(3):
        for way, moves_y in enumerate(ways):
            at = p * n_ways + way
            for c in range(cells):
                proj[at * cells + c] = project(lines[way], p, c, a, in_t)
            window(zrow, [spots(lines[way], p, base, by_j)] * 3, cells)
            for r in range(3):
                there = [zrow[d, r : r + cells, :] for d in range(3)]
                moves = ((1 - p,), moves_y, (r - 1,))
                rads[at * 3 + r], wgts[at * 3 + r] = pair_terms(there, own_rows(own, cells), moves, None)
    acc[...] = jnp.zeros(acc.shape, F32)

    def step(at, carry):
        units = [unit(rads, wgts, proj, c, at * 3 + r, at * cells + c + r - 1) for c, r in inside(cells)]
        add_pairs(units, cells, lanes, w1, w2, acc, k, f)
        return carry

    lax.fori_loop(0, 3 * n_ways, step, 0)


def last_kernel(sizes, ways, counts_ref, *refs):
    cells, a, f, k = sizes
    lows, highs, refs = refs[: len(ways)], refs[len(ways) : 2 * len(ways)], refs[2 * len(ways) :]
    packed, own, w1, w2, in_t, by_j, pick, dense_w, final_w, biases, acc0, acc1, acc2 = refs[:13]
    out_ref, acc, proj, rads, wgts = refs[13:]
    lanes, base, n_ways = a * a, cells * a, len(ways)
    coords = own_rows(own, cells)
    units = []
    for p in range(3):
        for way, moves_y in enumerate(ways):
            for high in range(2):
                block, cell, c, r = (highs[way], 0, cells - 1, 2) if high else (lows[way], cells - 1, 0, 0)
                at = (p * n_ways + way) * 2 + high
                proj[at] = project(block, p, cell, a, in_t)
                table = spots(block, p, base, by_j)
                there = [table[d * cells + cell : d * cells + cell + 1] for d in range(3)]
                here = [coords[d][c : c + 1] for d in range(3)]
                moves = ((1 - p,), moves_y, (r - 1,))
                rads[at], wgts[at] = pair_terms(there, here, moves, None)
                units.append((
                    c, lambda at=at: rads[at], lambda at=at: wgts[at], lambda at=at: proj[at],
                ))
    acc[...] = acc0[...] + acc1[...] + acc2[...]
    add_pairs(units, cells, lanes, w1, w2, acc, k, f)

    messages = []
    for c in range(cells):
        head, tail = split_bf16(acc[c], 2)
        messages.append(
            lax.dot_general(pick[...], head, NT, preferred_element_type=F32)
            + lax.dot_general(pick[...], tail, NT, preferred_element_type=F32)
        )
    message = jnp.concatenate(messages, axis=0).astype(BF16)
    inner = jnp.dot(message, dense_w[...], preferred_element_type=F32) + biases[0:1, :]
    inner = (jax.nn.softplus(inner) - LOG_TWO).astype(BF16)
    update = jnp.dot(inner, final_w[...], preferred_element_type=F32) + biases[1:2, :]
    slot = lax.broadcasted_iota(jnp.int32, (a, f), 0)
    for c in range(cells):
        here = packed[c * a : (c + 1) * a, :].astype(F32)
        value = here + update[c * a : (c + 1) * a]
        out_ref[c] = jnp.where(slot < counts_ref[c], value, 0.0).astype(BF16)


def shifted(value, steps):
    axes = [axis for axis, s in steps if s % lax.axis_size(axis)]
    if not axes:
        return value
    sizes = [lax.axis_size(axis) for axis in axes]
    moves = [dict(steps)[axis] for axis in axes]
    pairs = []
    for at in np.ndindex(*sizes):
        to = [(i + s) % n for i, s, n in zip(at, moves, sizes)]
        pairs.append((int(np.ravel_multi_index(at, sizes)), int(np.ravel_multi_index(to, sizes))))
    return lax.ppermute(value, tuple(axes), pairs)


def on_chip(value):
    return pltpu.with_memory_space_constraint(value, pltpu.VMEM)


def shards(
    atoms,
    places,
    counts,
    in_weight,
    basis_weight,
    basis_bias,
    filter_weight,
    filter_bias,
    dense_weight,
    dense_bias,
    final_weight,
    final_bias,
):
    cells_x, cells_y, cells_z, a, f = atoms.shape
    assert cells_x == 1 and cells_y == 1
    cells = cells_z
    k = basis_weight.shape[0]
    lanes = a * a
    sizes = (cells, a, f, k)
    vmem = pl.BlockSpec(memory_space=pltpu.VMEM)
    smem = pl.BlockSpec(memory_space=pltpu.SMEM)
    counts = counts.reshape(cells)
    packed = pl.pallas_call(
        pack_kernel,
        out_shape=pltpu.VMEM((cells * a + 16, f), BF16),
        in_specs=[smem, vmem, vmem],
        out_specs=vmem,
    )(counts, atoms.reshape(cells, a, f), jnp.swapaxes(places, 2, 3).reshape(3, cells, a))
    above = shifted(packed, [("gx", -1)])
    below = shifted(packed, [("gx", 1)])
    sums = pltpu.VMEM((cells, f, lanes), F32)
    row = pltpu.VMEM((3, 16, lanes), F32)

    def call(kernel, out_shape, scratch, args, scalars=()):
        single = not isinstance(out_shape, list)
        return pl.pallas_call(
            kernel,
            out_shape=out_shape,
            in_specs=[smem] * len(scalars) + [vmem] * len(args),
            out_specs=vmem if single else [vmem] * len(out_shape),
            scratch_shapes=scratch,
            cost_estimate=pl.CostEstimate(flops=10**9, transcendentals=10**6, bytes_accessed=10**6),
        )(*scalars, *args)

    def tiles(n):
        return pltpu.VMEM((n, f, 128), F32)

    def terms(n, rows):
        return [pltpu.VMEM((n, rows, lanes), F32)] * 2

    acc0, w1, w2, in_t, dense_w, final_w, biases, by_j, pick, own = call(
        lambda *refs: first_kernel(sizes, *refs),
        [
            sums,
            pltpu.VMEM((f, PAD_K + EXTRA), BF16),
            pltpu.VMEM((f, f + EXTRA), BF16),
            pltpu.VMEM((f, f), BF16),
            pltpu.VMEM((f, f), BF16),
            pltpu.VMEM((f, f), BF16),
            pltpu.VMEM((2, f), F32),
            pltpu.VMEM((f, lanes), BF16),
            pltpu.VMEM((a, lanes), BF16),
            pltpu.VMEM((16, lanes), F32),
        ],
        [tiles(cells), row] + terms(3, cells),
        (
            on_chip(packed),
            in_weight,
            basis_weight,
            basis_bias.reshape(1, f),
            filter_weight,
            filter_bias.reshape(1, f),
            dense_weight,
            dense_bias.reshape(1, f),
            final_weight,
            final_bias.reshape(1, f),
        ),
    )
    above, below, acc0 = lax.optimization_barrier((above, below, acc0))
    line = jnp.stack([above, packed, below])

    y_steps, ways = ([1], [(1, -1)]) if lax.axis_size("gy") == 2 else ([1, -1], [(1,), (-1,)])
    z_steps = [1] if lax.axis_size("gz") == 2 else [-1, 1]
    y_lines = [shifted(line, [("gy", -y)]) for y in y_steps]
    near_z = [shifted(line, [("gz", -z)]) for z in z_steps]

    n_ways = len(ways)
    shared = tuple(map(on_chip, (own, w1, w2, in_t, by_j)))
    acc1 = call(
        lambda *refs: near_kernel(sizes, *refs),
        sums,
        [tiles(3 * (cells + 2)), row] + terms(9, cells),
        (on_chip(line), on_chip(near_z[0]), on_chip(near_z[-1])) + shared,
    )
    y_lines, acc1 = lax.optimization_barrier((y_lines, acc1))
    far_z = [[shifted(y_line, [("gz", -z)]) for z in z_steps] for y_line in y_lines]
    acc2 = call(
        lambda *refs: plane_kernel(sizes, ways, *refs),
        sums,
        [tiles(3 * n_ways * cells), row] + terms(9 * n_ways, cells),
        tuple(map(on_chip, y_lines)) + shared,
    )
    far_z, acc2 = lax.optimization_barrier((far_z, acc2))
    out = call(
        lambda *refs: last_kernel(sizes, ways, *refs),
        jax.ShapeDtypeStruct((cells, a, f), BF16),
        [sums, tiles(6 * n_ways)] + terms(6 * n_ways, 1),
        tuple(map(on_chip, [z[0] for z in far_z] + [z[-1] for z in far_z] + [packed]))
        + shared
        + tuple(map(on_chip, (pick, dense_w, final_w, biases, acc0, acc1, acc2))),
        (counts,),
    )
    return out.reshape(atoms.shape)


def solution(mesh):
    placed = (
        P(("groups", "gx"), "gy", "gz", None, None),
        P(("groups", "gx"), "gy", "gz", None, None),
        P(("groups", "gx"), "gy", "gz"),
    ) + (P(),) * 9
    return jax.shard_map(
        shards,
        mesh=mesh,
        in_specs=placed,
        out_specs=P(("groups", "gx"), "gy", "gz", None, None),
        check_vma=False,
    )
```

```python
import math

import jax
import jax.numpy as jnp
import numpy as np
from jax import lax
from jax.experimental import pallas as pl
from jax.experimental.pallas import tpu as pltpu
from jax.sharding import PartitionSpec as P

LOG_TWO = 0.6931471805599453
LOG2_E = 1.4426950408889634
BASIS_GAMMA = 10.0
CELL_EDGE = 5.0
GAP_SCALE = math.sqrt(BASIS_GAMMA * LOG2_E)
FAR = 8.0
PAD_K = 64
EXTRA = 16

COS_SERIES = [(-1.0) ** m * (math.pi / 2) ** (2 * m) / math.factorial(2 * m) for m in range(9)]
F32, BF16 = jnp.float32, jnp.bfloat16
NT = (((1,), (1,)), ((), ()))


def split_bf16(values, parts):
    out = []
    rest = values
    for _ in range(parts):
        head = rest.astype(BF16)
        out.append(head)
        rest = rest - head.astype(F32)
    return out


def pack_kernel(counts_ref, atoms_ref, places_ref, out_ref):
    cells, a, f = atoms_ref.shape
    for c in range(cells):
        out_ref[c * a : (c + 1) * a, :] = atoms_ref[c]
    cell = lax.broadcasted_iota(jnp.int32, (cells, a), 0)
    slot = lax.broadcasted_iota(jnp.int32, (cells, a), 1)
    filled = jnp.zeros((cells, a), jnp.int32)
    for c in range(cells):
        filled = jnp.where(cell == c, counts_ref[c], filled)
    out_ref[cells * a :, :] = jnp.zeros((out_ref.shape[0] - cells * a, f), BF16)
    spots = [jnp.where(slot < filled, places_ref[d].astype(F32), FAR) for d in range(3)]
    table = jnp.concatenate(spots, axis=0)
    out_ref[cells * a : cells * a + 3 * cells, :a] = table.astype(BF16)


def spread(a, lanes, rows, by_j):
    row = lax.broadcasted_iota(jnp.int32, (rows, lanes), 0)
    lane = lax.broadcasted_iota(jnp.int32, (1, lanes), 1)
    return (row == (lane % a if by_j else lane // a)).astype(F32).astype(BF16)


def project(block, p, c, a, in_t):
    rows = block[p, c * a : (c + 1) * a, :]
    return lax.dot_general(in_t[...], jnp.concatenate([rows] * (128 // a), axis=0), NT, preferred_element_type=F32)


def spots(block, p, base, by_j):
    return jnp.dot(block[p, base : base + 16, :], by_j[...], preferred_element_type=F32)


def pair_terms(there, own, moves, drop):
    square = None
    for d, move in enumerate(moves):
        gap = there[d] - own[d]
        if len(move) == 2:
            gap = jnp.minimum(jnp.abs(gap + 1.0), jnp.abs(gap - 1.0))
        else:
            gap = gap + float(move[0])
        square = gap * gap if square is None else square + gap * gap
    far = jnp.sqrt(square)
    cosine = jnp.full(square.shape, COS_SERIES[-1], F32)
    for term in COS_SERIES[-2::-1]:
        cosine = cosine * square + term
    keep = CELL_EDGE * far < CELL_EDGE
    if drop is not None:
        keep = keep & drop
    return far * (CELL_EDGE * GAP_SCALE), jnp.where(keep, cosine * cosine * LOG_TWO, 0.0)


def add_pairs(units, cells, lanes, w1, w2, acc, k, f, start=None):
    reps = lanes // 128
    centers = lax.broadcasted_iota(jnp.int32, (PAD_K, 128), 0).astype(F32)
    centers = centers * (GAP_SCALE * CELL_EDGE / (k - 1))
    centers = jnp.concatenate([centers] * reps, axis=1)
    ones = jnp.ones((EXTRA, lanes), BF16)
    totals = [None] * cells
    left = [sum(u[0] == c for u in units) for c in range(cells)]
    first, second = {}, {}
    for n in range(len(units) + 2):
        if n < len(units):
            gap = units[n][1]() - centers
            grid = jnp.exp2(gap * -gap).astype(BF16)
            first[n] = jnp.dot(w1[...], jnp.concatenate([grid, ones], axis=0), preferred_element_type=F32)
        if 0 <= n - 1 < len(units):
            hidden = jnp.log2(jnp.exp2(first.pop(n - 1)) + 0.5).astype(BF16)
            weight = jnp.broadcast_to(units[n - 1][2](), (EXTRA, lanes)).astype(BF16)
            hidden = (hidden.reshape(f // EXTRA, EXTRA, lanes) * weight[None]).reshape(f, lanes)
            second[n - 1] = jnp.dot(w2[...], jnp.concatenate([hidden, weight], axis=0), preferred_element_type=F32)
        if 0 <= n - 2 < len(units):
            c = units[n - 2][0]
            term = second.pop(n - 2) * jnp.concatenate([units[n - 2][3]()] * reps, axis=1)
            totals[c] = term if totals[c] is None else totals[c] + term
            left[c] -= 1
            if left[c] == 0:
                acc[c] = totals[c] + (acc if start is None else start)[c]


def unit(rads, wgts, proj, c, at, cell):
    return (c, lambda: rads[at, c : c + 1, :], lambda: wgts[at, c : c + 1, :], lambda: proj[cell])


def inside(cells):
    return [(c, r) for c in range(cells) for r in range(3) if 0 <= c + r - 1 < cells]


def window(zrow, tables, cells):
    for d in range(3):
        low, mid, high = (t[d * cells : (d + 1) * cells] for t in tables)
        zrow[d, 1 + cells : 1 + 2 * cells, :] = high
        zrow[d, 1 : 1 + cells, :] = mid
        zrow[d, 0:1, :] = low[cells - 1 : cells]


def own_rows(own, cells):
    return [own[d * cells : (d + 1) * cells, :] for d in range(3)]


def first_kernel(
    sizes, counts_ref, packed, in_w, basis_w, basis_b, filt_w, filt_b, dense_w, dense_b, final_w, final_b,
    acc, w1, w2, in_t, dense_o, final_o, biases, by_j, pick, own, filled, proj, zrow, rads, wgts
):
    cells, a, f, k = sizes
    lanes, base = a * a, cells * a
    w1[...] = jnp.zeros(w1.shape, BF16)
    w1[:, :k] = (basis_w[...].astype(F32).T * LOG2_E).astype(BF16)
    bias = (basis_b[...] * LOG2_E - 1.0).T
    for n, part in enumerate(split_bf16(bias, 3)):
        w1[:, PAD_K + n : PAD_K + n + 1] = part
    w2[...] = jnp.zeros(w2.shape, BF16)
    w2[:, :f] = filt_w[...].astype(F32).T.astype(BF16)
    for n, part in enumerate(split_bf16(filt_b[...].T * LOG2_E, 2)):
        w2[:, f + n : f + n + 1] = part
    in_t[...] = in_w[...].astype(F32).T.astype(BF16)
    dense_o[...] = dense_w[...]
    final_o[...] = final_w[...]
    biases[0:1, :] = dense_b[...]
    biases[1:2, :] = final_b[...]
    slot = lax.broadcasted_iota(jnp.int32, (a, f), 0)
    for c in range(cells):
        filled[c * a : (c + 1) * a, :] = (slot < counts_ref[c]).astype(F32)
    by_j[...] = spread(a, lanes, f, True)
    pick[...] = spread(a, lanes, a, False)
    line = packed.reshape(1, *packed.shape)
    own[...] = spots(line, 0, base, spread(a, lanes, f, False))
    table = spots(line, 0, base, by_j)
    window(zrow, (table, table, table), cells)
    small = lax.broadcasted_iota(jnp.int32, (1, lanes), 1)
    other = small % a != small // a
    for c in range(cells):
        proj[c] = project(line, 0, c, a, in_t)
    for r in range(3):
        there = [zrow[d, r : r + cells, :] for d in range(3)]
        moves = ((0,), (0,), (r - 1,))
        rads[r], wgts[r] = pair_terms(there, own_rows(own, cells), moves, other if r == 1 else None)
    acc[...] = jnp.zeros(acc.shape, F32)
    units = [unit(rads, wgts, proj, c, r, c + r - 1) for c, r in inside(cells)]
    add_pairs(units, cells, lanes, w1, w2, acc, k, f)


def near_kernel(sizes, line, low_line, high_line, own, w1, w2, in_t, by_j, acc0, acc, proj, zrow, rads, wgts):
    cells, a, f, k = sizes
    lanes, base, wide = a * a, cells * a, cells + 2
    for p in range(3):
        proj[p * wide] = project(low_line, p, cells - 1, a, in_t)
        proj[p * wide + cells + 1] = project(high_line, p, 0, a, in_t)
        for c in range(cells if p != 1 else 0):
            proj[p * wide + c + 1] = project(line, p, c, a, in_t)
        window(zrow, [spots(l, p, base, by_j) for l in (low_line, line, high_line)], cells)
        for r in range(3):
            there = [zrow[d, r : r + cells, :] for d in range(3)]
            moves = ((1 - p,), (0,), (r - 1,))
            rads[p * 3 + r], wgts[p * 3 + r] = pair_terms(there, own_rows(own, cells), moves, None)
    for p in range(3):
        spans = [(c, r) for c in range(cells) for r in range(3)] if p != 1 else [(0, 0), (cells - 1, 2)]
        units = [unit(rads, wgts, proj, c, p * 3 + r, p * wide + c + r) for c, r in spans]
        add_pairs(units, cells, lanes, w1, w2, acc, k, f, acc0 if p == 0 else None)


def plane_kernel(sizes, ways, *refs):
    cells, a, f, k = sizes
    lines, refs = refs[: len(ways)], refs[len(ways) :]
    own, w1, w2, in_t, by_j, acc1, acc, proj, zrow, rads, wgts = refs
    lanes, base, n_ways = a * a, cells * a, len(ways)
    for p in range(3):
        for way, moves_y in enumerate(ways):
            at = p * n_ways + way
            for c in range(cells):
                proj[at * cells + c] = project(lines[way], p, c, a, in_t)
            window(zrow, [spots(lines[way], p, base, by_j)] * 3, cells)
            for r in range(3):
                there = [zrow[d, r : r + cells, :] for d in range(3)]
                moves = ((1 - p,), moves_y, (r - 1,))
                rads[at * 3 + r], wgts[at * 3 + r] = pair_terms(there, own_rows(own, cells), moves, None)
    for at in range(3 * n_ways):
        units = [unit(rads, wgts, proj, c, at * 3 + r, at * cells + c + r - 1) for c, r in inside(cells)]
        add_pairs(units, cells, lanes, w1, w2, acc, k, f, acc1 if at == 0 else None)


def last_kernel(sizes, ways, *refs):
    cells, a, f, k = sizes
    lows, highs, refs = refs[: len(ways)], refs[len(ways) : 2 * len(ways)], refs[2 * len(ways) :]
    packed, own, w1, w2, in_t, by_j, pick, dense_w, final_w, biases, filled, acc2 = refs[:12]
    out_ref, acc, proj, rads, wgts = refs[12:]
    lanes, base, n_ways = a * a, cells * a, len(ways)
    coords = own_rows(own, cells)
    units = []
    for p in range(3):
        for way, moves_y in enumerate(ways):
            for high in range(2):
                block, cell, c, r = (highs[way], 0, cells - 1, 2) if high else (lows[way], cells - 1, 0, 0)
                at = (p * n_ways + way) * 2 + high
                proj[at] = project(block, p, cell, a, in_t)
                table = spots(block, p, base, by_j)
                there = [table[d * cells + cell : d * cells + cell + 1] for d in range(3)]
                here = [coords[d][c : c + 1] for d in range(3)]
                moves = ((1 - p,), moves_y, (r - 1,))
                rads[at], wgts[at] = pair_terms(there, here, moves, None)
                units.append((
                    c, lambda at=at: rads[at], lambda at=at: wgts[at], lambda at=at: proj[at],
                ))
    units.sort(key=lambda u: u[0])
    add_pairs(units, cells, lanes, w1, w2, acc, k, f, acc2)

    messages = []
    for c in range(cells):
        head = (acc if c in (0, cells - 1) else acc2)[c].astype(BF16)
        messages.append(lax.dot_general(pick[...], head, NT, preferred_element_type=F32))
    message = jnp.concatenate(messages, axis=0).astype(BF16)
    inner = jnp.dot(message, dense_w[...], preferred_element_type=F32) + biases[0:1, :]
    inner = (jax.nn.softplus(inner) - LOG_TWO).astype(BF16)
    update = jnp.dot(inner, final_w[...], preferred_element_type=F32) + biases[1:2, :]
    value = (packed[: cells * a, :].astype(F32) + update) * filled[...]
    for c in range(cells):
        out_ref[c] = value[c * a : (c + 1) * a].astype(BF16)


def shifted(value, steps):
    axes = [axis for axis, s in steps if s % lax.axis_size(axis)]
    if not axes:
        return value
    sizes = [lax.axis_size(axis) for axis in axes]
    moves = [dict(steps)[axis] for axis in axes]
    pairs = []
    for at in np.ndindex(*sizes):
        to = [(i + s) % n for i, s, n in zip(at, moves, sizes)]
        pairs.append((int(np.ravel_multi_index(at, sizes)), int(np.ravel_multi_index(to, sizes))))
    return lax.ppermute(value, tuple(axes), pairs)


def on_chip(value):
    return pltpu.with_memory_space_constraint(value, pltpu.VMEM)


def shards(
    atoms,
    places,
    counts,
    in_weight,
    basis_weight,
    basis_bias,
    filter_weight,
    filter_bias,
    dense_weight,
    dense_bias,
    final_weight,
    final_bias,
):
    cells_x, cells_y, cells_z, a, f = atoms.shape
    assert cells_x == 1 and cells_y == 1
    cells = cells_z
    k = basis_weight.shape[0]
    lanes = a * a
    sizes = (cells, a, f, k)
    vmem = pl.BlockSpec(memory_space=pltpu.VMEM)
    smem = pl.BlockSpec(memory_space=pltpu.SMEM)
    counts = counts.reshape(cells)
    packed = pl.pallas_call(
        pack_kernel,
        out_shape=pltpu.VMEM((cells * a + 16, f), BF16),
        in_specs=[smem, vmem, vmem],
        out_specs=vmem,
    )(counts, atoms.reshape(cells, a, f), jnp.swapaxes(places, 2, 3).reshape(3, cells, a))
    above = shifted(packed, [("gx", -1)])
    below = shifted(packed, [("gx", 1)])
    sums = pltpu.VMEM((cells, f, lanes), F32)
    row = pltpu.VMEM((3, 16, lanes), F32)

    def call(kernel, out_shape, scratch, args, scalars=()):
        single = not isinstance(out_shape, list)
        return pl.pallas_call(
            kernel,
            out_shape=out_shape,
            in_specs=[smem] * len(scalars) + [vmem] * len(args),
            out_specs=vmem if single else [vmem] * len(out_shape),
            scratch_shapes=scratch,
            cost_estimate=pl.CostEstimate(flops=10**9, transcendentals=10**6, bytes_accessed=10**6),
        )(*scalars, *args)

    def tiles(n):
        return pltpu.VMEM((n, f, 128), F32)

    def terms(n, rows):
        return [pltpu.VMEM((n, rows, lanes), F32)] * 2

    acc0, w1, w2, in_t, dense_w, final_w, biases, by_j, pick, own, filled = call(
        lambda *refs: first_kernel(sizes, *refs),
        [
            sums,
            pltpu.VMEM((f, PAD_K + EXTRA), BF16),
            pltpu.VMEM((f, f + EXTRA), BF16),
            pltpu.VMEM((f, f), BF16),
            pltpu.VMEM((f, f), BF16),
            pltpu.VMEM((f, f), BF16),
            pltpu.VMEM((2, f), F32),
            pltpu.VMEM((f, lanes), BF16),
            pltpu.VMEM((a, lanes), BF16),
            pltpu.VMEM((16, lanes), F32),
            pltpu.VMEM((cells * a, f), F32),
        ],
        [tiles(cells), row] + terms(3, cells),
        (
            on_chip(packed),
            in_weight,
            basis_weight,
            basis_bias.reshape(1, f),
            filter_weight,
            filter_bias.reshape(1, f),
            dense_weight,
            dense_bias.reshape(1, f),
            final_weight,
            final_bias.reshape(1, f),
        ),
        (counts,),
    )
    above, below, acc0 = lax.optimization_barrier((above, below, acc0))
    line = jnp.stack([above, packed, below])

    y_steps, ways = ([1], [(1, -1)]) if lax.axis_size("gy") == 2 else ([1, -1], [(1,), (-1,)])
    z_steps = [1] if lax.axis_size("gz") == 2 else [-1, 1]
    y_lines = [shifted(line, [("gy", -y)]) for y in y_steps]
    near_z = [shifted(line, [("gz", -z)]) for z in z_steps]

    n_ways = len(ways)
    shared = tuple(map(on_chip, (own, w1, w2, in_t, by_j)))
    acc1 = call(
        lambda *refs: near_kernel(sizes, *refs),
        sums,
        [tiles(3 * (cells + 2)), row] + terms(9, cells),
        (on_chip(line), on_chip(near_z[0]), on_chip(near_z[-1])) + shared + (on_chip(acc0),),
    )
    y_lines, acc1 = lax.optimization_barrier((y_lines, acc1))
    far_z = [[shifted(y_line, [("gz", -z)]) for z in z_steps] for y_line in y_lines]
    acc2 = call(
        lambda *refs: plane_kernel(sizes, ways, *refs),
        sums,
        [tiles(3 * n_ways * cells), row] + terms(9 * n_ways, cells),
        tuple(map(on_chip, y_lines)) + shared + (on_chip(acc1),),
    )
    far_z, acc2 = lax.optimization_barrier((far_z, acc2))
    out = call(
        lambda *refs: last_kernel(sizes, ways, *refs),
        jax.ShapeDtypeStruct((cells, a, f), BF16),
        [sums, tiles(6 * n_ways)] + terms(6 * n_ways, 1),
        tuple(map(on_chip, [z[0] for z in far_z] + [z[-1] for z in far_z] + [packed]))
        + shared
        + tuple(map(on_chip, (pick, dense_w, final_w, biases, filled, acc2))),
    )
    return out.reshape(atoms.shape)


def solution(mesh):
    placed = (
        P(("groups", "gx"), "gy", "gz", None, None),
        P(("groups", "gx"), "gy", "gz", None, None),
        P(("groups", "gx"), "gy", "gz"),
    ) + (P(),) * 9
    return jax.shard_map(
        shards,
        mesh=mesh,
        in_specs=placed,
        out_specs=P(("groups", "gx"), "gy", "gz", None, None),
        check_vma=False,
    )
```

```python
import math

import jax
import jax.numpy as jnp
import numpy as np
from jax import lax
from jax.experimental import pallas as pl
from jax.experimental.pallas import tpu as pltpu
from jax.sharding import PartitionSpec as P

LOG_TWO = 0.6931471805599453
LOG2_E = 1.4426950408889634
BASIS_GAMMA = 10.0
CELL_EDGE = 5.0
GAP_SCALE = math.sqrt(BASIS_GAMMA * LOG2_E)
FAR = 8.0
PAD_K = 64
EXTRA = 16

COS_SERIES = [(-1.0) ** m * (math.pi / 2) ** (2 * m) / math.factorial(2 * m) for m in range(9)]
F32, BF16 = jnp.float32, jnp.bfloat16
NT = (((1,), (1,)), ((), ()))


def split_bf16(values, parts):
    out = []
    rest = values
    for _ in range(parts):
        head = rest.astype(BF16)
        out.append(head)
        rest = rest - head.astype(F32)
    return out


def pack_kernel(counts_ref, atoms_ref, places_ref, out_ref):
    cells, a, f = atoms_ref.shape
    for c in range(cells):
        out_ref[c * a : (c + 1) * a, :] = atoms_ref[c]
    cell = lax.broadcasted_iota(jnp.int32, (cells, a), 0)
    slot = lax.broadcasted_iota(jnp.int32, (cells, a), 1)
    filled = jnp.zeros((cells, a), jnp.int32)
    for c in range(cells):
        filled = jnp.where(cell == c, counts_ref[c], filled)
    out_ref[cells * a :, :] = jnp.zeros((out_ref.shape[0] - cells * a, f), BF16)
    spots = [jnp.where(slot < filled, places_ref[d].astype(F32), FAR) for d in range(3)]
    table = jnp.concatenate(spots, axis=0)
    out_ref[cells * a : cells * a + 3 * cells, :a] = table.astype(BF16)


def spread(a, lanes, rows, by_j):
    row = lax.broadcasted_iota(jnp.int32, (rows, lanes), 0)
    lane = lax.broadcasted_iota(jnp.int32, (1, lanes), 1)
    return (row == (lane % a if by_j else lane // a)).astype(F32).astype(BF16)


def project(proj, slots, in_t, a):
    reps = 128 // a
    f = in_t.shape[0]
    lane = lax.broadcasted_iota(jnp.int32, (1, 128), 1) % a
    for n in range(0, len(slots), reps):
        some = slots[n : n + reps]
        rows = [block[p, c * a : (c + 1) * a, :] for _, block, p, c in some]
        rows = jnp.concatenate(rows + rows[-1:] * (reps - len(rows)), axis=0)
        tile = lax.dot_general(in_t[...], rows, NT, preferred_element_type=F32)
        for m, (at, _, _, _) in enumerate(some):
            proj[at] = jnp.take_along_axis(tile, jnp.broadcast_to(lane + m * a, (f, 128)), axis=1)


def spots(block, p, base, by_j):
    return jnp.dot(block[p, base : base + 16, :], by_j[...], preferred_element_type=F32)


def pair_terms(there, own, moves, drop):
    square = None
    for d, move in enumerate(moves or ((), (), ())):
        gap = there[d] if own is None else there[d] - own[d]
        if len(move) == 0:
            pass
        elif len(move) == 2:
            gap = jnp.minimum(jnp.abs(gap + 1.0), jnp.abs(gap - 1.0))
        else:
            gap = gap + float(move[0])
        square = gap * gap if square is None else square + gap * gap
    far = jnp.sqrt(square)
    cosine = jnp.full(square.shape, COS_SERIES[-1], F32)
    for term in COS_SERIES[-2::-1]:
        cosine = cosine * square + term
    keep = CELL_EDGE * far < CELL_EDGE
    if drop is not None:
        keep = keep & drop
    return far * (CELL_EDGE * GAP_SCALE), jnp.where(keep, cosine * cosine * LOG_TWO, 0.0)


def add_pairs(units, cells, lanes, w1, w2, acc, k, f, start=None):
    reps = lanes // 128
    centers = lax.broadcasted_iota(jnp.int32, (PAD_K, 128), 0).astype(F32)
    centers = centers * (GAP_SCALE * CELL_EDGE / (k - 1))
    centers = jnp.concatenate([centers] * reps, axis=1)
    ones = jnp.ones((EXTRA, lanes), BF16)
    total, opened = None, set()
    first, second = {}, {}
    for n in range(len(units) + 2):
        if n < len(units):
            gap = units[n][1]() - centers
            grid = jnp.exp2(gap * -gap).astype(BF16)
            first[n] = jnp.dot(w1[...], jnp.concatenate([grid, ones], axis=0), preferred_element_type=F32)
        if 0 <= n - 1 < len(units):
            hidden = jnp.log2(jnp.exp2(first.pop(n - 1)) + 0.5).astype(BF16)
            weight = jnp.broadcast_to(units[n - 1][2](), (EXTRA, lanes)).astype(BF16)
            hidden = (hidden.reshape(f // EXTRA, EXTRA, lanes) * weight[None]).reshape(f, lanes)
            second[n - 1] = jnp.dot(w2[...], jnp.concatenate([hidden, weight], axis=0), preferred_element_type=F32)
        if 0 <= n - 2 < len(units):
            c = units[n - 2][0]
            term = second.pop(n - 2) * jnp.concatenate([units[n - 2][3]()] * reps, axis=1)
            total = term if total is None else total + term
            if n - 1 == len(units) or units[n - 1][0] != c:
                acc[c] = total + (acc if start is None or c in opened else start)[c]
                total = None
                opened.add(c)


def unit(rads, wgts, proj, c, at, cell):
    return (c, lambda: rads[at, c : c + 1, :], lambda: wgts[at, c : c + 1, :], lambda: proj[cell])


def inside(cells):
    return [(c, r) for c in range(cells) for r in range(3) if 0 <= c + r - 1 < cells]


def window(zrow, tables, cells):
    for d in range(3):
        low, mid, high = (t[d * cells : (d + 1) * cells] for t in tables)
        zrow[d, 1 + cells : 1 + 2 * cells, :] = high
        zrow[d, 1 : 1 + cells, :] = mid
        zrow[d, 0:1, :] = low[cells - 1 : cells]


def own_rows(own, cells):
    return [own[d * cells : (d + 1) * cells, :] for d in range(3)]


def first_kernel(
    sizes, counts_ref, packed, in_w, basis_w, basis_b, filt_w, filt_b, dense_w, dense_b, final_w, final_b,
    acc, w1, w2, in_t, dense_o, final_o, biases, by_j, pick, own, filled, proj, zrow, rads, wgts
):
    cells, a, f, k = sizes
    lanes, base = a * a, cells * a
    w1[...] = jnp.zeros(w1.shape, BF16)
    w1[:, :k] = (basis_w[...].astype(F32).T * LOG2_E).astype(BF16)
    bias = (basis_b[...] * LOG2_E - 1.0).T
    for n, part in enumerate(split_bf16(bias, 3)):
        w1[:, PAD_K + n : PAD_K + n + 1] = part
    w2[...] = jnp.zeros(w2.shape, BF16)
    w2[:, :f] = filt_w[...].astype(F32).T.astype(BF16)
    for n, part in enumerate(split_bf16(filt_b[...].T * LOG2_E, 2)):
        w2[:, f + n : f + n + 1] = part
    in_t[...] = in_w[...].astype(F32).T.astype(BF16)
    dense_o[...] = dense_w[...]
    final_o[...] = final_w[...]
    biases[0:1, :] = dense_b[...]
    biases[1:2, :] = final_b[...]
    slot = lax.broadcasted_iota(jnp.int32, (a, f), 0)
    for c in range(cells):
        filled[c * a : (c + 1) * a, :] = (slot < counts_ref[c]).astype(F32)
    by_j[...] = spread(a, lanes, f, True)
    pick[...] = spread(a, lanes, a, False)
    line = packed.reshape(1, *packed.shape)
    own[...] = spots(line, 0, base, spread(a, lanes, f, False))
    table = spots(line, 0, base, by_j)
    window(zrow, (table, table, table), cells)
    small = lax.broadcasted_iota(jnp.int32, (1, lanes), 1)
    other = small % a != small // a
    project(proj, [(c, line, 0, c) for c in range(cells)], in_t, a)
    for r in range(3):
        there = [zrow[d, r : r + cells, :] for d in range(3)]
        moves = ((0,), (0,), (r - 1,))
        rads[r], wgts[r] = pair_terms(there, own_rows(own, cells), moves, other if r == 1 else None)
    acc[...] = jnp.zeros(acc.shape, F32)
    units = [unit(rads, wgts, proj, c, r, c + r - 1) for c, r in inside(cells)]
    add_pairs(units, cells, lanes, w1, w2, acc, k, f)


def near_kernel(sizes, line, low_line, high_line, own, w1, w2, in_t, by_j, acc0, acc, proj, zrow, rads, wgts):
    cells, a, f, k = sizes
    lanes, base, wide = a * a, cells * a, cells + 2
    slots = []
    for p in range(3):
        slots += [(p * wide, low_line, p, cells - 1), (p * wide + cells + 1, high_line, p, 0)]
        slots += [(p * wide + c + 1, line, p, c) for c in range(cells if p != 1 else 0)]
        window(zrow, [spots(l, p, base, by_j) for l in (low_line, line, high_line)], cells)
        for r in range(3):
            there = [zrow[d, r : r + cells, :] for d in range(3)]
            moves = ((1 - p,), (0,), (r - 1,))
            rads[p * 3 + r], wgts[p * 3 + r] = pair_terms(there, own_rows(own, cells), moves, None)
    project(proj, slots, in_t, a)
    units = []
    for p in range(3):
        spans = [(c, r) for c in range(cells) for r in range(3)] if p != 1 else [(0, 0), (cells - 1, 2)]
        units += [unit(rads, wgts, proj, c, p * 3 + r, p * wide + c + r) for c, r in spans]
    units.sort(key=lambda u: u[0])
    add_pairs(units, cells, lanes, w1, w2, acc, k, f, acc0)


def plane_kernel(sizes, ways, *refs):
    cells, a, f, k = sizes
    lines, refs = refs[: len(ways)], refs[len(ways) :]
    own, w1, w2, in_t, by_j, acc1, acc, proj, zrow, rads, wgts = refs
    lanes, base, n_ways = a * a, cells * a, len(ways)
    slots = []
    for p in range(3):
        for way, moves_y in enumerate(ways):
            at = p * n_ways + way
            slots += [(at * cells + c, lines[way], p, c) for c in range(cells)]
            window(zrow, [spots(lines[way], p, base, by_j)] * 3, cells)
            for r in range(3):
                there = [zrow[d, r : r + cells, :] for d in range(3)]
                moves = ((1 - p,), moves_y, (r - 1,))
                rads[at * 3 + r], wgts[at * 3 + r] = pair_terms(there, own_rows(own, cells), moves, None)
    project(proj, slots, in_t, a)
    units = []
    for at in range(3 * n_ways):
        units += [unit(rads, wgts, proj, c, at * 3 + r, at * cells + c + r - 1) for c, r in inside(cells)]
    units.sort(key=lambda u: u[0])
    add_pairs(units, cells, lanes, w1, w2, acc, k, f, acc1)


def last_kernel(sizes, ways, sides, *refs):
    cells, a, f, k = sizes
    lows, highs = refs[: len(ways)], refs[(sides - 1) * len(ways) : sides * len(ways)]
    refs = refs[sides * len(ways) :]
    packed, own, w1, w2, in_t, by_j, pick, dense_w, final_w, biases, filled, acc2 = refs[:12]
    out_ref, acc, proj, gaps, rads, wgts = refs[12:]
    lanes, base, n_ways = a * a, cells * a, len(ways)
    coords = own_rows(own, cells)
    edge = [(p, way, high) for p in range(3) for way in range(n_ways) for high in range(2)]
    count = len(edge)
    slots, units = [], []
    stacked = [jnp.concatenate([block[p, base : base + 16, :] for p in range(3)], axis=0) for block in lows]
    low_rows = [jnp.dot(rows, by_j[...], preferred_element_type=F32) for rows in stacked]
    if highs[0] is lows[0]:
        high_rows = low_rows
    else:
        stacked = [jnp.concatenate([block[p, base : base + 16, :] for p in range(3)], axis=0) for block in highs]
        high_rows = [jnp.dot(rows, by_j[...], preferred_element_type=F32) for rows in stacked]
    for at, (p, way, high) in enumerate(edge):
        block, cell, c = (highs[way], 0, cells - 1) if high else (lows[way], cells - 1, 0)
        slots.append((at, block, p, cell))
        table = (high_rows if high else low_rows)[way]
        for d in range(3):
            row = p * 16 + d * cells + cell
            gaps[d, at : at + 1, :] = table[row : row + 1] - coords[d][c : c + 1]
        units.append((
            c, lambda at=at: rads[at : at + 1, :], lambda at=at: wgts[at : at + 1, :], lambda at=at: proj[at],
        ))
    project(proj, slots, in_t, a)
    index = lax.broadcasted_iota(jnp.int32, (count, lanes), 0)

    def per_row(value):
        out = jnp.zeros((count, lanes), F32)
        for at, key in enumerate(edge):
            if value(*key):
                out = jnp.where(index == at, float(value(*key)), out)
        return out

    gap = [gaps[d, 0:count, :] for d in range(3)]
    gap[0] = gap[0] + per_row(lambda p, way, high: 1 - p)
    gap[2] = gap[2] + per_row(lambda p, way, high: 2 * high - 1)
    if n_ways == 1:
        gap[1] = jnp.minimum(jnp.abs(gap[1] + 1.0), jnp.abs(gap[1] - 1.0))
    else:
        gap[1] = gap[1] + per_row(lambda p, way, high: ways[way][0])
    rads[...], wgts[...] = pair_terms(gap, None, None, None)
    units.sort(key=lambda u: u[0])
    add_pairs(units, cells, lanes, w1, w2, acc, k, f, acc2)

    messages = []
    for c in range(cells):
        head = (acc if c in (0, cells - 1) else acc2)[c].astype(BF16)
        messages.append(lax.dot_general(pick[...], head, NT, preferred_element_type=F32))
    message = jnp.concatenate(messages, axis=0).astype(BF16)
    inner = jnp.dot(message, dense_w[...], preferred_element_type=F32) + biases[0:1, :]
    inner = (jnp.maximum(inner, 0.0) + jnp.log(0.5 + 0.5 * jnp.exp(-jnp.abs(inner)))).astype(BF16)
    update = jnp.dot(inner, final_w[...], preferred_element_type=F32) + biases[1:2, :]
    value = (packed[: cells * a, :].astype(F32) + update) * filled[...]
    for c in range(cells):
        out_ref[c] = value[c * a : (c + 1) * a].astype(BF16)


def shifted(value, steps):
    axes = [axis for axis, s in steps if s % lax.axis_size(axis)]
    if not axes:
        return value
    sizes = [lax.axis_size(axis) for axis in axes]
    moves = [dict(steps)[axis] for axis in axes]
    pairs = []
    for at in np.ndindex(*sizes):
        to = [(i + s) % n for i, s, n in zip(at, moves, sizes)]
        pairs.append((int(np.ravel_multi_index(at, sizes)), int(np.ravel_multi_index(to, sizes))))
    return lax.ppermute(value, tuple(axes), pairs)


def on_chip(value):
    return pltpu.with_memory_space_constraint(value, pltpu.VMEM)


def shards(
    atoms,
    places,
    counts,
    in_weight,
    basis_weight,
    basis_bias,
    filter_weight,
    filter_bias,
    dense_weight,
    dense_bias,
    final_weight,
    final_bias,
):
    cells_x, cells_y, cells_z, a, f = atoms.shape
    assert cells_x == 1 and cells_y == 1
    cells = cells_z
    k = basis_weight.shape[0]
    lanes = a * a
    sizes = (cells, a, f, k)
    vmem = pl.BlockSpec(memory_space=pltpu.VMEM)
    smem = pl.BlockSpec(memory_space=pltpu.SMEM)
    counts = counts.reshape(cells)
    packed = pl.pallas_call(
        pack_kernel,
        out_shape=pltpu.VMEM((cells * a + 16, f), BF16),
        in_specs=[smem, vmem, vmem],
        out_specs=vmem,
    )(counts, atoms.reshape(cells, a, f), jnp.swapaxes(places, 2, 3).reshape(3, cells, a))
    above = shifted(packed, [("gx", -1)])
    below = shifted(packed, [("gx", 1)])
    sums = pltpu.VMEM((cells, f, lanes), F32)
    row = pltpu.VMEM((3, 16, lanes), F32)

    def call(kernel, out_shape, scratch, args, scalars=()):
        single = not isinstance(out_shape, list)
        return pl.pallas_call(
            kernel,
            out_shape=out_shape,
            in_specs=[smem] * len(scalars) + [vmem] * len(args),
            out_specs=vmem if single else [vmem] * len(out_shape),
            scratch_shapes=scratch,
            cost_estimate=pl.CostEstimate(flops=10**9, transcendentals=10**6, bytes_accessed=10**6),
        )(*scalars, *args)

    def tiles(n):
        return pltpu.VMEM((n, f, 128), F32)

    def terms(n, rows):
        return [pltpu.VMEM((n, rows, lanes), F32)] * 2

    acc0, w1, w2, in_t, dense_w, final_w, biases, by_j, pick, own, filled = call(
        lambda *refs: first_kernel(sizes, *refs),
        [
            sums,
            pltpu.VMEM((f, PAD_K + EXTRA), BF16),
            pltpu.VMEM((f, f + EXTRA), BF16),
            pltpu.VMEM((f, f), BF16),
            pltpu.VMEM((f, f), BF16),
            pltpu.VMEM((f, f), BF16),
            pltpu.VMEM((2, f), F32),
            pltpu.VMEM((f, lanes), BF16),
            pltpu.VMEM((a, lanes), BF16),
            pltpu.VMEM((16, lanes), F32),
            pltpu.VMEM((cells * a, f), F32),
        ],
        [tiles(cells), row] + terms(3, cells),
        (
            on_chip(packed),
            in_weight,
            basis_weight,
            basis_bias.reshape(1, f),
            filter_weight,
            filter_bias.reshape(1, f),
            dense_weight,
            dense_bias.reshape(1, f),
            final_weight,
            final_bias.reshape(1, f),
        ),
        (counts,),
    )
    above, below, acc0 = lax.optimization_barrier((above, below, acc0))
    line = jnp.stack([above, packed, below])

    y_steps, ways = ([1], [(1, -1)]) if lax.axis_size("gy") == 2 else ([1, -1], [(1,), (-1,)])
    z_steps = [1] if lax.axis_size("gz") == 2 else [-1, 1]
    y_lines = [shifted(line, [("gy", -y)]) for y in y_steps]
    near_z = [shifted(line, [("gz", -z)]) for z in z_steps]

    n_ways = len(ways)
    shared = tuple(map(on_chip, (own, w1, w2, in_t, by_j)))
    acc1 = call(
        lambda *refs: near_kernel(sizes, *refs),
        sums,
        [tiles(3 * (cells + 2)), row] + terms(9, cells),
        (on_chip(line), on_chip(near_z[0]), on_chip(near_z[-1])) + shared + (on_chip(acc0),),
    )
    y_lines, acc1 = lax.optimization_barrier((y_lines, acc1))
    far_z = [[shifted(y_line, [("gz", -z)]) for z in z_steps] for y_line in y_lines]
    acc2 = call(
        lambda *refs: plane_kernel(sizes, ways, *refs),
        sums,
        [tiles(3 * n_ways * cells), row] + terms(9 * n_ways, cells),
        tuple(map(on_chip, y_lines)) + shared + (on_chip(acc1),),
    )
    far_z, acc2 = lax.optimization_barrier((far_z, acc2))
    out = call(
        lambda *refs: last_kernel(sizes, ways, len(z_steps), *refs),
        jax.ShapeDtypeStruct((cells, a, f), BF16),
        [sums, tiles(6 * n_ways), pltpu.VMEM((3, 8 * n_ways, lanes), F32)]
        + [pltpu.VMEM((6 * n_ways, lanes), F32)] * 2,
        tuple(map(on_chip, [z[side] for side in range(len(z_steps)) for z in far_z] + [packed]))
        + shared
        + tuple(map(on_chip, (pick, dense_w, final_w, biases, filled, acc2))),
    )
    return out.reshape(atoms.shape)


def solution(mesh):
    placed = (
        P(("groups", "gx"), "gy", "gz", None, None),
        P(("groups", "gx"), "gy", "gz", None, None),
        P(("groups", "gx"), "gy", "gz"),
    ) + (P(),) * 9
    return jax.shard_map(
        shards,
        mesh=mesh,
        in_specs=placed,
        out_specs=P(("groups", "gx"), "gy", "gz", None, None),
        check_vma=False,
    )
```

```python
import math

import jax
import jax.numpy as jnp
import numpy as np
from jax import lax
from jax.experimental import pallas as pl
from jax.experimental.pallas import tpu as pltpu
from jax.sharding import PartitionSpec as P

LOG_TWO = 0.6931471805599453
LOG2_E = 1.4426950408889634
BASIS_GAMMA = 10.0
CELL_EDGE = 5.0
GAP_SCALE = math.sqrt(BASIS_GAMMA * LOG2_E)
FAR = 8.0
PAD_K = 64
SLOTS = 16
SPOT_ROWS = 8
EXTRA = 16

COS_SERIES = [(-1.0) ** m * (math.pi / 2) ** (2 * m) / math.factorial(2 * m) for m in range(9)]
F32, BF16 = jnp.float32, jnp.bfloat16
NT = (((1,), (1,)), ((), ()))


def split_bf16(values, parts):
    out = []
    rest = values
    for _ in range(parts):
        head = rest.astype(BF16)
        out.append(head)
        rest = rest - head.astype(F32)
    return out


def pack_kernel(counts_ref, atoms_ref, places_ref, out_ref):
    cells, a, f = atoms_ref.shape
    for c in range(cells):
        out_ref[c * a : (c + 1) * a, :] = atoms_ref[c]
    cell = lax.broadcasted_iota(jnp.int32, (cells, a), 0)
    slot = lax.broadcasted_iota(jnp.int32, (cells, a), 1)
    filled = jnp.full((cells, a), counts_ref[0], jnp.int32)
    for c in range(1, cells):
        filled = jnp.where(cell == c, counts_ref[c], filled)
    out_ref[cells * a :, :] = jnp.zeros((out_ref.shape[0] - cells * a, f), BF16)
    spots = [jnp.where(slot < filled, places_ref[d].astype(F32), FAR) for d in range(3)]
    table = jnp.concatenate(spots, axis=0)
    for n in range(0, 3 * cells, SPOT_ROWS):
        rows, at = table[n : n + SPOT_ROWS], n // SPOT_ROWS * a
        out_ref[cells * a : cells * a + rows.shape[0], at : at + a] = rows.astype(BF16)


def spread(a, lanes, rows, by_j, groups=1):
    row = lax.broadcasted_iota(jnp.int32, (rows, groups * lanes), 0)
    lane = lax.broadcasted_iota(jnp.int32, (1, groups * lanes), 1)
    inner = lane % lanes
    slot = (inner % a if by_j else inner // a) + lane // lanes * a
    return (row == slot).astype(F32).astype(BF16)


def spot_groups(cells):
    return -(-3 * cells // SPOT_ROWS)


def project(proj, slots, in_t, a):
    reps = 128 // a
    f = in_t.shape[0]
    lane = lax.broadcasted_iota(jnp.int32, (1, 128), 1) % a
    for n in range(0, len(slots), reps):
        some = slots[n : n + reps]
        rows = [block[p, c * a : (c + 1) * a, :] for _, block, p, c in some]
        rows = jnp.concatenate(rows + rows[-1:] * (reps - len(rows)), axis=0)
        tile = lax.dot_general(in_t[...], rows, NT, preferred_element_type=F32)
        for m, (at, _, _, _) in enumerate(some):
            proj[at] = jnp.take_along_axis(tile, jnp.broadcast_to(lane + m * a, (f, 128)), axis=1)


def spots(block, p, base, by_j):
    table = jnp.dot(block[p, base : base + SPOT_ROWS, :], by_j[...], preferred_element_type=F32)
    lanes = by_j.shape[1] // spot_groups(base // SLOTS)
    return jnp.concatenate([table[:, n : n + lanes] for n in range(0, table.shape[1], lanes)], axis=0)


def pair_terms(there, own, moves, drop):
    square = None
    for d, move in enumerate(moves or ((), (), ())):
        gap = there[d] if own is None else there[d] - own[d]
        if len(move) == 0:
            pass
        elif len(move) == 2:
            gap = jnp.minimum(jnp.abs(gap + 1.0), jnp.abs(gap - 1.0))
        else:
            gap = gap + float(move[0])
        square = gap * gap if square is None else square + gap * gap
    far = jnp.sqrt(square)
    cosine = jnp.full(square.shape, COS_SERIES[-1], F32)
    for term in COS_SERIES[-2::-1]:
        cosine = cosine * square + term
    keep = CELL_EDGE * far < CELL_EDGE
    if drop is not None:
        keep = keep & drop
    return far * (CELL_EDGE * GAP_SCALE), jnp.where(keep, cosine * cosine * LOG_TWO, 0.0)


def add_pairs(units, cells, lanes, w1, w2, acc, k, f, start=None):
    reps = lanes // 128
    centers = lax.broadcasted_iota(jnp.int32, (PAD_K, 128), 0).astype(F32)
    centers = centers * (GAP_SCALE * CELL_EDGE / (k - 1))
    centers = jnp.concatenate([centers] * reps, axis=1)
    ones = jnp.ones((EXTRA, lanes), BF16)
    total, opened = None, set()
    first, second = {}, {}
    for n in range(len(units) + 2):
        if n < len(units):
            gap = units[n][1]() - centers
            grid = jnp.exp2(gap * -gap).astype(BF16)
            first[n] = jnp.dot(w1[...], jnp.concatenate([grid, ones], axis=0), preferred_element_type=F32)
        if 0 <= n - 1 < len(units):
            hidden = jnp.log2(jnp.exp2(first.pop(n - 1)) + 0.5).astype(BF16)
            weight = jnp.broadcast_to(units[n - 1][2](), (EXTRA, lanes)).astype(BF16)
            hidden = (hidden.reshape(f // EXTRA, EXTRA, lanes) * weight[None]).reshape(f, lanes)
            second[n - 1] = jnp.dot(w2[...], jnp.concatenate([hidden, weight], axis=0), preferred_element_type=F32)
        if 0 <= n - 2 < len(units):
            c = units[n - 2][0]
            term = second.pop(n - 2) * jnp.concatenate([units[n - 2][3]()] * reps, axis=1)
            total = term if total is None else total + term
            if n - 1 == len(units) or units[n - 1][0] != c:
                acc[c] = total + (acc if start is None or c in opened else start)[c]
                total = None
                opened.add(c)


def unit(rads, wgts, proj, c, at, cell):
    return (c, lambda: rads[at, c : c + 1, :], lambda: wgts[at, c : c + 1, :], lambda: proj[cell])


def inside(cells):
    return [(c, r) for c in range(cells) for r in range(3) if 0 <= c + r - 1 < cells]


def window(zrow, tables, cells):
    for d in range(3):
        low, mid, high = (t[d * cells : (d + 1) * cells] for t in tables)
        zrow[d, 1 + cells : 1 + 2 * cells, :] = high
        zrow[d, 1 : 1 + cells, :] = mid
        zrow[d, 0:1, :] = low[cells - 1 : cells]


def own_rows(own, cells):
    return [own[d * cells : (d + 1) * cells, :] for d in range(3)]


def first_kernel(
    sizes, counts_ref, packed, in_w, basis_w, basis_b, filt_w, filt_b, dense_w, dense_b, final_w, final_b,
    acc, w1, w2, in_t, dense_o, final_o, biases, by_j, pick, own, filled, proj, zrow, rads, wgts
):
    cells, a, f, k = sizes
    lanes, base = a * a, cells * a
    w1[...] = jnp.zeros(w1.shape, BF16)
    w1[:, :k] = (basis_w[...].astype(F32).T * LOG2_E).astype(BF16)
    bias = (basis_b[...] * LOG2_E - 1.0).T
    for n, part in enumerate(split_bf16(bias, 3)):
        w1[:, PAD_K + n : PAD_K + n + 1] = part
    w2[...] = jnp.zeros(w2.shape, BF16)
    w2[:, :f] = filt_w[...].astype(F32).T.astype(BF16)
    for n, part in enumerate(split_bf16(filt_b[...].T * LOG2_E, 2)):
        w2[:, f + n : f + n + 1] = part
    in_t[...] = in_w[...].astype(F32).T.astype(BF16)
    dense_o[...] = dense_w[...]
    final_o[...] = final_w[...]
    biases[0:1, :] = dense_b[...]
    biases[1:2, :] = final_b[...]
    slot = lax.broadcasted_iota(jnp.int32, (a, f), 0)
    for c in range(cells):
        filled[c * a : (c + 1) * a, :] = (slot < counts_ref[c]).astype(F32)
    by_j[...] = spread(a, lanes, f, True, spot_groups(cells))
    pick[...] = spread(a, lanes, a, False)
    line = packed.reshape(1, *packed.shape)
    own[...] = spots(line, 0, base, spread(a, lanes, f, False, spot_groups(cells)))
    table = spots(line, 0, base, by_j)
    window(zrow, (table, table, table), cells)
    small = lax.broadcasted_iota(jnp.int32, (1, lanes), 1)
    other = small % a != small // a
    project(proj, [(c, line, 0, c) for c in range(cells)], in_t, a)
    for r in range(3):
        there = [zrow[d, r : r + cells, :] for d in range(3)]
        moves = ((0,), (0,), (r - 1,))
        rads[r], wgts[r] = pair_terms(there, own_rows(own, cells), moves, other if r == 1 else None)
    acc[...] = jnp.zeros(acc.shape, F32)
    units = [unit(rads, wgts, proj, c, r, c + r - 1) for c, r in inside(cells)]
    add_pairs(units, cells, lanes, w1, w2, acc, k, f)


def near_kernel(sizes, line, low_line, high_line, own, w1, w2, in_t, by_j, acc0, acc, proj, zrow, rads, wgts):
    cells, a, f, k = sizes
    lanes, base, wide = a * a, cells * a, cells + 2
    slots = []
    for p in range(3):
        slots += [(p * wide, low_line, p, cells - 1), (p * wide + cells + 1, high_line, p, 0)]
        slots += [(p * wide + c + 1, line, p, c) for c in range(cells if p != 1 else 0)]
        window(zrow, [spots(l, p, base, by_j) for l in (low_line, line, high_line)], cells)
        for r in range(3):
            there = [zrow[d, r : r + cells, :] for d in range(3)]
            moves = ((1 - p,), (0,), (r - 1,))
            rads[p * 3 + r], wgts[p * 3 + r] = pair_terms(there, own_rows(own, cells), moves, None)
    project(proj, slots, in_t, a)
    units = []
    for p in range(3):
        spans = [(c, r) for c in range(cells) for r in range(3)] if p != 1 else [(0, 0), (cells - 1, 2)]
        units += [unit(rads, wgts, proj, c, p * 3 + r, p * wide + c + r) for c, r in spans]
    units.sort(key=lambda u: u[0])
    add_pairs(units, cells, lanes, w1, w2, acc, k, f, acc0)


def plane_kernel(sizes, ways, *refs):
    cells, a, f, k = sizes
    lines, refs = refs[: len(ways)], refs[len(ways) :]
    own, w1, w2, in_t, by_j, acc1, acc, proj, zrow, rads, wgts = refs
    lanes, base, n_ways = a * a, cells * a, len(ways)
    slots = []
    for p in range(3):
        for way, moves_y in enumerate(ways):
            at = p * n_ways + way
            slots += [(at * cells + c, lines[way], p, c) for c in range(cells)]
            window(zrow, [spots(lines[way], p, base, by_j)] * 3, cells)
            for r in range(3):
                there = [zrow[d, r : r + cells, :] for d in range(3)]
                moves = ((1 - p,), moves_y, (r - 1,))
                rads[at * 3 + r], wgts[at * 3 + r] = pair_terms(there, own_rows(own, cells), moves, None)
    project(proj, slots, in_t, a)
    units = []
    for at in range(3 * n_ways):
        units += [unit(rads, wgts, proj, c, at * 3 + r, at * cells + c + r - 1) for c, r in inside(cells)]
    units.sort(key=lambda u: u[0])
    add_pairs(units, cells, lanes, w1, w2, acc, k, f, acc1)


def last_kernel(sizes, ways, sides, *refs):
    cells, a, f, k = sizes
    lows, highs = refs[: len(ways)], refs[(sides - 1) * len(ways) : sides * len(ways)]
    refs = refs[sides * len(ways) :]
    packed, own, w1, w2, in_t, by_j, pick, dense_w, final_w, biases, filled, acc2 = refs[:12]
    out_ref, acc, proj, gaps, rads, wgts = refs[12:]
    lanes, base, n_ways = a * a, cells * a, len(ways)
    coords = own_rows(own, cells)
    edge = [(p, way, high) for p in range(3) for way in range(n_ways) for high in range(2)]
    count = len(edge)
    slots, units = [], []
    low_rows = [[spots(block, p, base, by_j) for p in range(3)] for block in lows]
    high_rows = low_rows
    if highs[0] is not lows[0]:
        high_rows = [[spots(block, p, base, by_j) for p in range(3)] for block in highs]
    for at, (p, way, high) in enumerate(edge):
        block, cell, c = (highs[way], 0, cells - 1) if high else (lows[way], cells - 1, 0)
        slots.append((at, block, p, cell))
        table = (high_rows if high else low_rows)[way][p]
        for d in range(3):
            row = d * cells + cell
            gaps[d, at : at + 1, :] = table[row : row + 1] - coords[d][c : c + 1]
        units.append((
            c, lambda at=at: rads[at : at + 1, :], lambda at=at: wgts[at : at + 1, :], lambda at=at: proj[at],
        ))
    project(proj, slots, in_t, a)
    index = lax.broadcasted_iota(jnp.int32, (count, lanes), 0)

    def per_row(value):
        out = jnp.zeros((count, lanes), F32)
        for at, key in enumerate(edge):
            if value(*key):
                out = jnp.where(index == at, float(value(*key)), out)
        return out

    gap = [gaps[d, 0:count, :] for d in range(3)]
    gap[0] = gap[0] + per_row(lambda p, way, high: 1 - p)
    gap[2] = gap[2] + per_row(lambda p, way, high: 2 * high - 1)
    if n_ways == 1:
        gap[1] = jnp.minimum(jnp.abs(gap[1] + 1.0), jnp.abs(gap[1] - 1.0))
    else:
        gap[1] = gap[1] + per_row(lambda p, way, high: ways[way][0])
    rads[...], wgts[...] = pair_terms(gap, None, None, None)
    units.sort(key=lambda u: u[0])
    add_pairs(units, cells, lanes, w1, w2, acc, k, f, acc2)

    messages = []
    for c in range(cells):
        head = (acc if c in (0, cells - 1) else acc2)[c].astype(BF16)
        messages.append(lax.dot_general(pick[...], head, NT, preferred_element_type=F32))
    message = jnp.concatenate(messages, axis=0).astype(BF16)
    inner = jnp.dot(message, dense_w[...], preferred_element_type=F32) + biases[0:1, :]
    inner = (jnp.maximum(inner, 0.0) + jnp.log(0.5 + 0.5 * jnp.exp(-jnp.abs(inner)))).astype(BF16)
    update = jnp.dot(inner, final_w[...], preferred_element_type=F32) + biases[1:2, :]
    value = (packed[: cells * a, :].astype(F32) + update) * filled[...]
    for c in range(cells):
        out_ref[c] = value[c * a : (c + 1) * a].astype(BF16)


def shifted(value, steps):
    axes = [axis for axis, s in steps if s % lax.axis_size(axis)]
    if not axes:
        return value
    sizes = [lax.axis_size(axis) for axis in axes]
    moves = [dict(steps)[axis] for axis in axes]
    pairs = []
    for at in np.ndindex(*sizes):
        to = [(i + s) % n for i, s, n in zip(at, moves, sizes)]
        pairs.append((int(np.ravel_multi_index(at, sizes)), int(np.ravel_multi_index(to, sizes))))
    return lax.ppermute(value, tuple(axes), pairs)


def on_chip(value):
    return pltpu.with_memory_space_constraint(value, pltpu.VMEM)


def shards(
    atoms,
    places,
    counts,
    in_weight,
    basis_weight,
    basis_bias,
    filter_weight,
    filter_bias,
    dense_weight,
    dense_bias,
    final_weight,
    final_bias,
):
    cells_x, cells_y, cells_z, a, f = atoms.shape
    assert cells_x == 1 and cells_y == 1 and a == SLOTS
    cells = cells_z
    k = basis_weight.shape[0]
    lanes = a * a
    sizes = (cells, a, f, k)
    vmem = pl.BlockSpec(memory_space=pltpu.VMEM)
    smem = pl.BlockSpec(memory_space=pltpu.SMEM)
    counts = counts.reshape(cells)
    packed = pl.pallas_call(
        pack_kernel,
        out_shape=pltpu.VMEM((cells * a + SPOT_ROWS, f), BF16),
        in_specs=[smem, vmem, vmem],
        out_specs=vmem,
    )(counts, atoms.reshape(cells, a, f), jnp.swapaxes(places, 2, 3).reshape(3, cells, a))
    above = shifted(packed, [("gx", -1)])
    below = shifted(packed, [("gx", 1)])
    sums = pltpu.VMEM((cells, f, lanes), F32)
    row = pltpu.VMEM((3, 16, lanes), F32)

    def call(kernel, out_shape, scratch, args, scalars=()):
        single = not isinstance(out_shape, list)
        return pl.pallas_call(
            kernel,
            out_shape=out_shape,
            in_specs=[smem] * len(scalars) + [vmem] * len(args),
            out_specs=vmem if single else [vmem] * len(out_shape),
            scratch_shapes=scratch,
            cost_estimate=pl.CostEstimate(flops=10**9, transcendentals=10**6, bytes_accessed=10**6),
        )(*scalars, *args)

    def tiles(n):
        return pltpu.VMEM((n, f, 128), F32)

    def terms(n, rows):
        return [pltpu.VMEM((n, rows, lanes), F32)] * 2

    acc0, w1, w2, in_t, dense_w, final_w, biases, by_j, pick, own, filled = call(
        lambda *refs: first_kernel(sizes, *refs),
        [
            sums,
            pltpu.VMEM((f, PAD_K + EXTRA), BF16),
            pltpu.VMEM((f, f + EXTRA), BF16),
            pltpu.VMEM((f, f), BF16),
            pltpu.VMEM((f, f), BF16),
            pltpu.VMEM((f, f), BF16),
            pltpu.VMEM((2, f), F32),
            pltpu.VMEM((f, spot_groups(cells) * lanes), BF16),
            pltpu.VMEM((a, lanes), BF16),
            pltpu.VMEM((16, lanes), F32),
            pltpu.VMEM((cells * a, f), F32),
        ],
        [tiles(cells), row] + terms(3, cells),
        (
            on_chip(packed),
            in_weight,
            basis_weight,
            basis_bias.reshape(1, f),
            filter_weight,
            filter_bias.reshape(1, f),
            dense_weight,
            dense_bias.reshape(1, f),
            final_weight,
            final_bias.reshape(1, f),
        ),
        (counts,),
    )
    above, below, acc0 = lax.optimization_barrier((above, below, acc0))
    line = jnp.stack([above, packed, below])

    y_steps, ways = ([1], [(1, -1)]) if lax.axis_size("gy") == 2 else ([1, -1], [(1,), (-1,)])
    z_steps = [1] if lax.axis_size("gz") == 2 else [-1, 1]
    y_lines = [shifted(line, [("gy", -y)]) for y in y_steps]
    near_z = [shifted(line, [("gz", -z)]) for z in z_steps]

    n_ways = len(ways)
    shared = tuple(map(on_chip, (own, w1, w2, in_t, by_j)))
    acc1 = call(
        lambda *refs: near_kernel(sizes, *refs),
        sums,
        [tiles(3 * (cells + 2)), row] + terms(9, cells),
        (on_chip(line), on_chip(near_z[0]), on_chip(near_z[-1])) + shared + (on_chip(acc0),),
    )
    y_lines, acc1 = lax.optimization_barrier((y_lines, acc1))
    far_z = [[shifted(y_line, [("gz", -z)]) for z in z_steps] for y_line in y_lines]
    acc2 = call(
        lambda *refs: plane_kernel(sizes, ways, *refs),
        sums,
        [tiles(3 * n_ways * cells), row] + terms(9 * n_ways, cells),
        tuple(map(on_chip, y_lines)) + shared + (on_chip(acc1),),
    )
    far_z, acc2 = lax.optimization_barrier((far_z, acc2))
    out = call(
        lambda *refs: last_kernel(sizes, ways, len(z_steps), *refs),
        jax.ShapeDtypeStruct((cells, a, f), BF16),
        [sums, tiles(6 * n_ways), pltpu.VMEM((3, 8 * n_ways, lanes), F32)]
        + [pltpu.VMEM((6 * n_ways, lanes), F32)] * 2,
        tuple(map(on_chip, [z[side] for side in range(len(z_steps)) for z in far_z] + [packed]))
        + shared
        + tuple(map(on_chip, (pick, dense_w, final_w, biases, filled, acc2))),
    )
    return out.reshape(atoms.shape)


def solution(mesh):
    placed = (
        P(("groups", "gx"), "gy", "gz", None, None),
        P(("groups", "gx"), "gy", "gz", None, None),
        P(("groups", "gx"), "gy", "gz"),
    ) + (P(),) * 9
    return jax.shard_map(
        shards,
        mesh=mesh,
        in_specs=placed,
        out_specs=P(("groups", "gx"), "gy", "gz", None, None),
        check_vma=False,
    )
```

```python
import math

import jax
import jax.numpy as jnp
import numpy as np
from jax import lax
from jax.experimental import pallas as pl
from jax.experimental.pallas import tpu as pltpu
from jax.sharding import PartitionSpec as P

LOG_TWO = 0.6931471805599453
LOG2_E = 1.4426950408889634
BASIS_GAMMA = 10.0
CELL_EDGE = 5.0
GAP_SCALE = math.sqrt(BASIS_GAMMA * LOG2_E)
FAR = 8.0
PAD_K = 56
SLOTS = 16
SPOT_ROWS = 8
EXTRA = 16

COS_SERIES = [(-1.0) ** m * (math.pi / 2) ** (2 * m) / math.factorial(2 * m) for m in range(9)]
F32, BF16 = jnp.float32, jnp.bfloat16
NT = (((1,), (1,)), ((), ()))


def split_bf16(values, parts):
    out = []
    rest = values
    for _ in range(parts):
        head = rest.astype(BF16)
        out.append(head)
        rest = rest - head.astype(F32)
    return out


def pack_kernel(counts_hbm, atoms_hbm, places_hbm, out_ref, counts_ref, places_ref, done):
    _, cells, a = places_ref.shape
    top = cells * a
    copies = [
        pltpu.make_async_copy(counts_hbm, counts_ref, done.at[0]),
        pltpu.make_async_copy(places_hbm, places_ref, done.at[1]),
        pltpu.make_async_copy(atoms_hbm, out_ref.at[0:top, :], done.at[2]),
    ]
    for copy in copies:
        copy.start()
    cell = lax.broadcasted_iota(jnp.int32, (cells, a), 0)
    slot = lax.broadcasted_iota(jnp.int32, (cells, a), 1)
    copies[0].wait()
    filled = jnp.full((cells, a), counts_ref[0], jnp.int32)
    for c in range(1, cells):
        filled = jnp.where(cell == c, counts_ref[c], filled)
    copies[1].wait()
    spots = [jnp.where(slot < filled, places_ref[d].astype(F32), FAR) for d in range(3)]
    table = jnp.concatenate(spots, axis=0)
    groups = [table[n : n + SPOT_ROWS] for n in range(0, 3 * cells, SPOT_ROWS)]
    short = SPOT_ROWS - groups[-1].shape[0]
    if short:
        groups[-1] = jnp.concatenate([groups[-1], jnp.zeros((short, a), F32)], axis=0)
    groups.append(jnp.zeros((SPOT_ROWS, out_ref.shape[1] - a * len(groups)), F32))
    out_ref[top:, :] = jnp.concatenate(groups, axis=1).astype(BF16)
    copies[2].wait()


def spread(a, lanes, rows, by_j, groups=1):
    row = lax.broadcasted_iota(jnp.int32, (rows, groups * lanes), 0)
    lane = lax.broadcasted_iota(jnp.int32, (1, groups * lanes), 1)
    inner = lane % lanes
    slot = (inner % a if by_j else inner // a) + lane // lanes * a
    return (row == slot).astype(F32).astype(BF16)


def spot_groups(cells):
    return -(-3 * cells // SPOT_ROWS)


def project(proj, slots, in_t, a):
    reps = 128 // a
    f = in_t.shape[0]
    lane = lax.broadcasted_iota(jnp.int32, (1, 128), 1) % a
    for n in range(0, len(slots), reps):
        some = slots[n : n + reps]
        rows = [block[p, c * a : (c + 1) * a, :] for _, block, p, c in some]
        rows = jnp.concatenate(rows + rows[-1:] * (reps - len(rows)), axis=0)
        tile = lax.dot_general(in_t[...], rows, NT, preferred_element_type=F32)
        for m, (at, _, _, _) in enumerate(some):
            proj[at] = jnp.take_along_axis(tile, jnp.broadcast_to(lane + m * a, (f, 128)), axis=1)


def spots(block, p, base, by_j):
    table = jnp.dot(block[p, base : base + SPOT_ROWS, :], by_j[...], preferred_element_type=F32)
    lanes = by_j.shape[1] // spot_groups(base // SLOTS)
    return jnp.concatenate([table[:, n : n + lanes] for n in range(0, table.shape[1], lanes)], axis=0)


def pair_terms(there, own, moves, drop):
    square = None
    for d, move in enumerate(moves or ((), (), ())):
        gap = there[d] if own is None else there[d] - own[d]
        if len(move) == 0:
            pass
        elif len(move) == 2:
            gap = jnp.minimum(jnp.abs(gap + 1.0), jnp.abs(gap - 1.0))
        else:
            gap = gap + float(move[0])
        square = gap * gap if square is None else square + gap * gap
    far = jnp.sqrt(square)
    cosine = jnp.full(square.shape, COS_SERIES[-1], F32)
    for term in COS_SERIES[-2::-1]:
        cosine = cosine * square + term
    keep = CELL_EDGE * far < CELL_EDGE
    if drop is not None:
        keep = keep & drop
    return far * (CELL_EDGE * GAP_SCALE), jnp.where(keep, cosine * cosine * LOG_TWO, 0.0)


def add_pairs(units, cells, lanes, w1, w2, acc, k, f, start=None):
    reps = lanes // 128
    centers = lax.broadcasted_iota(jnp.int32, (PAD_K, 128), 0).astype(F32)
    centers = centers * (GAP_SCALE * CELL_EDGE / (k - 1))
    centers = jnp.concatenate([centers] * reps, axis=1)
    ones = jnp.ones((8, lanes), F32)
    total, opened = None, set()
    for n, (c, radius, weight, tile) in enumerate(units):
        gap = radius() - centers
        grid = jnp.concatenate([jnp.exp2(gap * -gap), ones], axis=0).astype(BF16)
        hidden = jnp.dot(w1[...], grid, preferred_element_type=F32)
        hidden = jnp.log2(jnp.exp2(hidden) + 0.5).astype(BF16)
        scale = jnp.broadcast_to(weight(), (EXTRA, lanes)).astype(BF16)
        hidden = (hidden.reshape(f // EXTRA, EXTRA, lanes) * scale[None]).reshape(f, lanes)
        filt = jnp.dot(w2[...], jnp.concatenate([hidden, scale], axis=0), preferred_element_type=F32)
        term = filt * jnp.concatenate([tile()] * reps, axis=1)
        total = term if total is None else total + term
        if n + 1 == len(units) or units[n + 1][0] != c:
            acc[c] = total + (acc if start is None or c in opened else start)[c]
            total = None
            opened.add(c)


def unit(rads, wgts, proj, c, at, cell):
    return (c, lambda: rads[at, c : c + 1, :], lambda: wgts[at, c : c + 1, :], lambda: proj[cell])


def inside(cells):
    return [(c, r) for c in range(cells) for r in range(3) if 0 <= c + r - 1 < cells]


def window(zrow, tables, cells):
    for d in range(3):
        low, mid, high = (t[d * cells : (d + 1) * cells] for t in tables)
        zrow[d, 1 + cells : 1 + 2 * cells, :] = high
        zrow[d, 1 : 1 + cells, :] = mid
        zrow[d, 0:1, :] = low[cells - 1 : cells]


def own_rows(own, cells):
    return [own[d * cells : (d + 1) * cells, :] for d in range(3)]


def first_kernel(
    sizes, counts_ref, packed, in_w, basis_w, basis_b, filt_w, filt_b, dense_w, dense_b, final_w, final_b,
    acc, w1, w2, in_t, dense_o, final_o, biases, by_j, pick, own, filled, proj, zrow, rads, wgts
):
    cells, a, f, k = sizes
    lanes, base = a * a, cells * a
    w1[...] = jnp.zeros(w1.shape, BF16)
    w1[:, :k] = (basis_w[...].astype(F32).T * LOG2_E).astype(BF16)
    bias = (basis_b[...] * LOG2_E - 1.0).T
    for n, part in enumerate(split_bf16(bias, 3)):
        w1[:, PAD_K + n : PAD_K + n + 1] = part
    w2[...] = jnp.zeros(w2.shape, BF16)
    w2[:, :f] = filt_w[...].astype(F32).T.astype(BF16)
    for n, part in enumerate(split_bf16(filt_b[...].T * LOG2_E, 2)):
        w2[:, f + n : f + n + 1] = part
    in_t[...] = in_w[...].astype(F32).T.astype(BF16)
    dense_o[...] = dense_w[...]
    final_o[...] = final_w[...]
    biases[0:1, :] = dense_b[...]
    biases[1:2, :] = final_b[...]
    slot = lax.broadcasted_iota(jnp.int32, (a, f), 0)
    for c in range(cells):
        filled[c * a : (c + 1) * a, :] = (slot < counts_ref[c]).astype(F32)
    by_j[...] = spread(a, lanes, f, True, spot_groups(cells))
    pick[...] = spread(a, lanes, a, False)
    line = packed.reshape(1, *packed.shape)
    own[...] = spots(line, 0, base, spread(a, lanes, f, False, spot_groups(cells)))
    table = spots(line, 0, base, by_j)
    window(zrow, (table, table, table), cells)
    small = lax.broadcasted_iota(jnp.int32, (1, lanes), 1)
    other = small % a != small // a
    project(proj, [(c, line, 0, c) for c in range(cells)], in_t, a)
    for r in range(3):
        there = [zrow[d, r : r + cells, :] for d in range(3)]
        moves = ((0,), (0,), (r - 1,))
        rads[r], wgts[r] = pair_terms(there, own_rows(own, cells), moves, other if r == 1 else None)
    acc[...] = jnp.zeros(acc.shape, F32)
    units = [unit(rads, wgts, proj, c, r, c + r - 1) for c, r in inside(cells)]
    add_pairs(units, cells, lanes, w1, w2, acc, k, f)


def near_kernel(sizes, line, low_line, high_line, own, w1, w2, in_t, by_j, acc0, acc, proj, zrow, rads, wgts):
    cells, a, f, k = sizes
    lanes, base, wide = a * a, cells * a, cells + 2
    slots = []
    for p in range(3):
        slots += [(p * wide, low_line, p, cells - 1), (p * wide + cells + 1, high_line, p, 0)]
        slots += [(p * wide + c + 1, line, p, c) for c in range(cells if p != 1 else 0)]
        window(zrow, [spots(l, p, base, by_j) for l in (low_line, line, high_line)], cells)
        for r in range(3):
            there = [zrow[d, r : r + cells, :] for d in range(3)]
            moves = ((1 - p,), (0,), (r - 1,))
            rads[p * 3 + r], wgts[p * 3 + r] = pair_terms(there, own_rows(own, cells), moves, None)
    project(proj, slots, in_t, a)
    units = []
    for p in range(3):
        spans = [(c, r) for c in range(cells) for r in range(3)] if p != 1 else [(0, 0), (cells - 1, 2)]
        units += [unit(rads, wgts, proj, c, p * 3 + r, p * wide + c + r) for c, r in spans]
    units.sort(key=lambda u: u[0])
    add_pairs(units, cells, lanes, w1, w2, acc, k, f, acc0)


def plane_kernel(sizes, ways, *refs):
    cells, a, f, k = sizes
    lines, refs = refs[: len(ways)], refs[len(ways) :]
    own, w1, w2, in_t, by_j, acc1, acc, proj, zrow, rads, wgts = refs
    lanes, base, n_ways = a * a, cells * a, len(ways)
    slots = []
    for p in range(3):
        for way, moves_y in enumerate(ways):
            at = p * n_ways + way
            slots += [(at * cells + c, lines[way], p, c) for c in range(cells)]
            window(zrow, [spots(lines[way], p, base, by_j)] * 3, cells)
            for r in range(3):
                there = [zrow[d, r : r + cells, :] for d in range(3)]
                moves = ((1 - p,), moves_y, (r - 1,))
                rads[at * 3 + r], wgts[at * 3 + r] = pair_terms(there, own_rows(own, cells), moves, None)
    project(proj, slots, in_t, a)
    units = []
    for at in range(3 * n_ways):
        units += [unit(rads, wgts, proj, c, at * 3 + r, at * cells + c + r - 1) for c, r in inside(cells)]
    units.sort(key=lambda u: u[0])
    add_pairs(units, cells, lanes, w1, w2, acc, k, f, acc1)


def last_kernel(sizes, ways, sides, *refs):
    cells, a, f, k = sizes
    lows, highs = refs[: len(ways)], refs[(sides - 1) * len(ways) : sides * len(ways)]
    refs = refs[sides * len(ways) :]
    packed, own, w1, w2, in_t, by_j, pick, dense_w, final_w, biases, filled, acc2 = refs[:12]
    out_ref, acc, proj, gaps, rads, wgts = refs[12:]
    lanes, base, n_ways = a * a, cells * a, len(ways)
    coords = own_rows(own, cells)
    edge = [(p, way, high) for p in range(3) for way in range(n_ways) for high in range(2)]
    count = len(edge)
    slots, units = [], []
    low_rows = [[spots(block, p, base, by_j) for p in range(3)] for block in lows]
    high_rows = low_rows
    if highs[0] is not lows[0]:
        high_rows = [[spots(block, p, base, by_j) for p in range(3)] for block in highs]
    for at, (p, way, high) in enumerate(edge):
        block, cell, c = (highs[way], 0, cells - 1) if high else (lows[way], cells - 1, 0)
        slots.append((at, block, p, cell))
        table = (high_rows if high else low_rows)[way][p]
        for d in range(3):
            row = d * cells + cell
            gaps[d, at : at + 1, :] = table[row : row + 1] - coords[d][c : c + 1]
        units.append((
            c, lambda at=at: rads[at : at + 1, :], lambda at=at: wgts[at : at + 1, :], lambda at=at: proj[at],
        ))
    project(proj, slots, in_t, a)
    index = lax.broadcasted_iota(jnp.int32, (count, lanes), 0)

    def per_row(value):
        out = jnp.zeros((count, lanes), F32)
        for at, key in enumerate(edge):
            if value(*key):
                out = jnp.where(index == at, float(value(*key)), out)
        return out

    gap = [gaps[d, 0:count, :] for d in range(3)]
    gap[0] = gap[0] + per_row(lambda p, way, high: 1 - p)
    gap[2] = gap[2] + per_row(lambda p, way, high: 2 * high - 1)
    if n_ways == 1:
        gap[1] = jnp.minimum(jnp.abs(gap[1] + 1.0), jnp.abs(gap[1] - 1.0))
    else:
        gap[1] = gap[1] + per_row(lambda p, way, high: ways[way][0])
    rads[...], wgts[...] = pair_terms(gap, None, None, None)
    units.sort(key=lambda u: u[0])
    add_pairs(units, cells, lanes, w1, w2, acc, k, f, acc2)

    messages = []
    for c in range(cells):
        head = (acc if c in (0, cells - 1) else acc2)[c].astype(BF16)
        messages.append(lax.dot_general(pick[...], head, NT, preferred_element_type=F32))
    message = jnp.concatenate(messages, axis=0).astype(BF16)
    inner = jnp.dot(message, dense_w[...], preferred_element_type=F32) + biases[0:1, :]
    inner = (jnp.maximum(inner, 0.0) + jnp.log(0.5 + 0.5 * jnp.exp(-jnp.abs(inner)))).astype(BF16)
    update = jnp.dot(inner, final_w[...], preferred_element_type=F32) + biases[1:2, :]
    value = (packed[: cells * a, :].astype(F32) + update) * filled[...]
    for c in range(cells):
        out_ref[c] = value[c * a : (c + 1) * a].astype(BF16)


def shifted(value, steps):
    axes = [axis for axis, s in steps if s % lax.axis_size(axis)]
    if not axes:
        return value
    sizes = [lax.axis_size(axis) for axis in axes]
    moves = [dict(steps)[axis] for axis in axes]
    pairs = []
    for at in np.ndindex(*sizes):
        to = [(i + s) % n for i, s, n in zip(at, moves, sizes)]
        pairs.append((int(np.ravel_multi_index(at, sizes)), int(np.ravel_multi_index(to, sizes))))
    return lax.ppermute(value, tuple(axes), pairs)


def on_chip(value):
    return pltpu.with_memory_space_constraint(value, pltpu.VMEM)


def shards(
    atoms,
    places,
    counts,
    in_weight,
    basis_weight,
    basis_bias,
    filter_weight,
    filter_bias,
    dense_weight,
    dense_bias,
    final_weight,
    final_bias,
):
    cells_x, cells_y, cells_z, a, f = atoms.shape
    assert cells_x == 1 and cells_y == 1 and a == SLOTS
    cells = cells_z
    k = basis_weight.shape[0]
    lanes = a * a
    sizes = (cells, a, f, k)
    vmem = pl.BlockSpec(memory_space=pltpu.VMEM)
    smem = pl.BlockSpec(memory_space=pltpu.SMEM)
    counts = counts.reshape(cells)
    packed = pl.pallas_call(
        pack_kernel,
        out_shape=pltpu.VMEM((cells * a + SPOT_ROWS, f), BF16),
        in_specs=[pl.BlockSpec(memory_space=pl.ANY)] * 3,
        out_specs=vmem,
        scratch_shapes=[
            pltpu.SMEM((cells,), jnp.int32),
            pltpu.VMEM((3, cells, a), BF16),
            pltpu.SemaphoreType.DMA((3,)),
        ],
    )(counts, atoms.reshape(cells * a, f), jnp.swapaxes(places, 2, 3).reshape(3, cells, a))
    above = shifted(packed, [("gx", -1)])
    below = shifted(packed, [("gx", 1)])
    sums = pltpu.VMEM((cells, f, lanes), F32)
    row = pltpu.VMEM((3, 16, lanes), F32)

    def call(kernel, out_shape, scratch, args, scalars=()):
        single = not isinstance(out_shape, list)
        return pl.pallas_call(
            kernel,
            out_shape=out_shape,
            in_specs=[smem] * len(scalars) + [vmem] * len(args),
            out_specs=vmem if single else [vmem] * len(out_shape),
            scratch_shapes=scratch,
            cost_estimate=pl.CostEstimate(flops=10**9, transcendentals=10**6, bytes_accessed=10**6),
        )(*scalars, *args)

    def tiles(n):
        return pltpu.VMEM((n, f, 128), F32)

    def terms(n, rows):
        return [pltpu.VMEM((n, rows, lanes), F32)] * 2

    acc0, w1, w2, in_t, dense_w, final_w, biases, by_j, pick, own, filled = call(
        lambda *refs: first_kernel(sizes, *refs),
        [
            sums,
            pltpu.VMEM((f, PAD_K + 8), BF16),
            pltpu.VMEM((f, f + EXTRA), BF16),
            pltpu.VMEM((f, f), BF16),
            pltpu.VMEM((f, f), BF16),
            pltpu.VMEM((f, f), BF16),
            pltpu.VMEM((2, f), F32),
            pltpu.VMEM((f, spot_groups(cells) * lanes), BF16),
            pltpu.VMEM((a, lanes), BF16),
            pltpu.VMEM((16, lanes), F32),
            pltpu.VMEM((cells * a, f), F32),
        ],
        [tiles(cells), row] + terms(3, cells),
        (
            on_chip(packed),
            in_weight,
            basis_weight,
            basis_bias.reshape(1, f),
            filter_weight,
            filter_bias.reshape(1, f),
            dense_weight,
            dense_bias.reshape(1, f),
            final_weight,
            final_bias.reshape(1, f),
        ),
        (counts,),
    )
    above, below, acc0 = lax.optimization_barrier((above, below, acc0))
    line = jnp.stack([above, packed, below])

    y_steps, ways = ([1], [(1, -1)]) if lax.axis_size("gy") == 2 else ([1, -1], [(1,), (-1,)])
    z_steps = [1] if lax.axis_size("gz") == 2 else [-1, 1]
    y_lines = [shifted(line, [("gy", -y)]) for y in y_steps]
    near_z = [shifted(line, [("gz", -z)]) for z in z_steps]

    n_ways = len(ways)
    shared = tuple(map(on_chip, (own, w1, w2, in_t, by_j)))
    acc1 = call(
        lambda *refs: near_kernel(sizes, *refs),
        sums,
        [tiles(3 * (cells + 2)), row] + terms(9, cells),
        (on_chip(line), on_chip(near_z[0]), on_chip(near_z[-1])) + shared + (on_chip(acc0),),
    )
    y_lines, acc1 = lax.optimization_barrier((y_lines, acc1))
    far_z = [[shifted(y_line, [("gz", -z)]) for z in z_steps] for y_line in y_lines]
    acc2 = call(
        lambda *refs: plane_kernel(sizes, ways, *refs),
        sums,
        [tiles(3 * n_ways * cells), row] + terms(9 * n_ways, cells),
        tuple(map(on_chip, y_lines)) + shared + (on_chip(acc1),),
    )
    far_z, acc2 = lax.optimization_barrier((far_z, acc2))
    out = call(
        lambda *refs: last_kernel(sizes, ways, len(z_steps), *refs),
        jax.ShapeDtypeStruct((cells, a, f), BF16),
        [sums, tiles(6 * n_ways), pltpu.VMEM((3, 8 * n_ways, lanes), F32)]
        + [pltpu.VMEM((6 * n_ways, lanes), F32)] * 2,
        tuple(map(on_chip, [z[side] for side in range(len(z_steps)) for z in far_z] + [packed]))
        + shared
        + tuple(map(on_chip, (pick, dense_w, final_w, biases, filled, acc2))),
    )
    return out.reshape(atoms.shape)


def solution(mesh):
    placed = (
        P(("groups", "gx"), "gy", "gz", None, None),
        P(("groups", "gx"), "gy", "gz", None, None),
        P(("groups", "gx"), "gy", "gz"),
    ) + (P(),) * 9
    return jax.shard_map(
        shards,
        mesh=mesh,
        in_specs=placed,
        out_specs=P(("groups", "gx"), "gy", "gz", None, None),
        check_vma=False,
    )
```

```python
import math

import jax
import jax.numpy as jnp
import numpy as np
from jax import lax
from jax.experimental import pallas as pl
from jax.experimental.pallas import tpu as pltpu
from jax.sharding import PartitionSpec as P

LOG_TWO = 0.6931471805599453
LOG2_E = 1.4426950408889634
BASIS_GAMMA = 10.0
CELL_EDGE = 5.0
GAP_SCALE = math.sqrt(BASIS_GAMMA * LOG2_E)
FAR = 8.0
PAD_K = 56
SLOTS = 16
SPOT_ROWS = 8
EXTRA = 16

COS_SERIES = [(-1.0) ** m * (math.pi / 2) ** (2 * m) / math.factorial(2 * m) for m in range(9)]
F32, BF16 = jnp.float32, jnp.bfloat16
NT = (((1,), (1,)), ((), ()))


def split_bf16(values, parts):
    out = []
    rest = values
    for _ in range(parts):
        head = rest.astype(BF16)
        out.append(head)
        rest = rest - head.astype(F32)
    return out


def pack_kernel(counts_ref, atoms_ref, places_ref, out_ref):
    cells, a, f = atoms_ref.shape
    for c in range(cells):
        out_ref[c * a : (c + 1) * a, :] = atoms_ref[c]
    cell = lax.broadcasted_iota(jnp.int32, (cells, a), 0)
    slot = lax.broadcasted_iota(jnp.int32, (cells, a), 1)
    filled = jnp.full((cells, a), counts_ref[0], jnp.int32)
    for c in range(1, cells):
        filled = jnp.where(cell == c, counts_ref[c], filled)
    out_ref[cells * a :, :] = jnp.zeros((out_ref.shape[0] - cells * a, f), BF16)
    spots = [jnp.where(slot < filled, places_ref[d].astype(F32), FAR) for d in range(3)]
    table = jnp.concatenate(spots, axis=0)
    for n in range(0, 3 * cells, SPOT_ROWS):
        rows, at = table[n : n + SPOT_ROWS], n // SPOT_ROWS * a
        out_ref[cells * a : cells * a + rows.shape[0], at : at + a] = rows.astype(BF16)


def spread(a, lanes, rows, by_j, groups=1):
    row = lax.broadcasted_iota(jnp.int32, (rows, groups * lanes), 0)
    lane = lax.broadcasted_iota(jnp.int32, (1, groups * lanes), 1)
    inner = lane % lanes
    slot = (inner % a if by_j else inner // a) + lane // lanes * a
    return (row == slot).astype(F32).astype(BF16)


def spot_groups(cells):
    return -(-3 * cells // SPOT_ROWS)


def project(proj, slots, in_t, a):
    reps = 128 // a
    f = in_t.shape[0]
    lane = lax.broadcasted_iota(jnp.int32, (1, 128), 1) % a
    for n in range(0, len(slots), reps):
        some = slots[n : n + reps]
        rows = [block[p, c * a : (c + 1) * a, :] for _, block, p, c in some]
        rows = jnp.concatenate(rows + rows[-1:] * (reps - len(rows)), axis=0)
        tile = lax.dot_general(in_t[...], rows, NT, preferred_element_type=F32)
        for m, (at, _, _, _) in enumerate(some):
            proj[at] = jnp.take_along_axis(tile, jnp.broadcast_to(lane + m * a, (f, 128)), axis=1)


def spots(block, p, base, by_j):
    table = jnp.dot(block[p, base : base + SPOT_ROWS, :], by_j[...], preferred_element_type=F32)
    lanes = by_j.shape[1] // spot_groups(base // SLOTS)
    return jnp.concatenate([table[:, n : n + lanes] for n in range(0, table.shape[1], lanes)], axis=0)


def pair_terms(there, own, moves, drop):
    square = None
    for d, move in enumerate(moves or ((), (), ())):
        gap = there[d] if own is None else there[d] - own[d]
        if len(move) == 0:
            pass
        elif len(move) == 2:
            gap = jnp.minimum(jnp.abs(gap + 1.0), jnp.abs(gap - 1.0))
        else:
            gap = gap + float(move[0])
        square = gap * gap if square is None else square + gap * gap
    far = jnp.sqrt(square)
    cosine = jnp.full(square.shape, COS_SERIES[-1], F32)
    for term in COS_SERIES[-2::-1]:
        cosine = cosine * square + term
    keep = CELL_EDGE * far < CELL_EDGE
    if drop is not None:
        keep = keep & drop
    return far * (CELL_EDGE * GAP_SCALE), jnp.where(keep, cosine * cosine * LOG_TWO, 0.0)


def add_pairs(units, cells, lanes, w1, w2, acc, k, f, start=None):
    reps = lanes // 128
    centers = lax.broadcasted_iota(jnp.int32, (PAD_K, 128), 0).astype(F32)
    centers = centers * (GAP_SCALE * CELL_EDGE / (k - 1))
    centers = jnp.concatenate([centers] * reps, axis=1)
    ones = jnp.ones((8, lanes), F32)
    total, opened = None, set()
    for n, (c, radius, weight, tile) in enumerate(units):
        gap = radius() - centers
        grid = jnp.concatenate([jnp.exp2(gap * -gap), ones], axis=0).astype(BF16)
        hidden = jnp.dot(w1[...], grid, preferred_element_type=F32)
        hidden = jnp.log2(jnp.exp2(hidden) + 0.5).astype(BF16)
        scale = jnp.broadcast_to(weight(), (EXTRA, lanes)).astype(BF16)
        hidden = (hidden.reshape(f // EXTRA, EXTRA, lanes) * scale[None]).reshape(f, lanes)
        filt = jnp.dot(w2[...], jnp.concatenate([hidden, scale], axis=0), preferred_element_type=F32)
        term = filt * jnp.concatenate([tile()] * reps, axis=1)
        total = term if total is None else total + term
        if n + 1 == len(units) or units[n + 1][0] != c:
            acc[c] = total + (acc if start is None or c in opened else start)[c]
            total = None
            opened.add(c)


def unit(rads, wgts, proj, c, at, cell):
    return (c, lambda: rads[at, c : c + 1, :], lambda: wgts[at, c : c + 1, :], lambda: proj[cell])


def inside(cells):
    return [(c, r) for c in range(cells) for r in range(3) if 0 <= c + r - 1 < cells]


def window(zrow, tables, cells):
    for d in range(3):
        low, mid, high = (t[d * cells : (d + 1) * cells] for t in tables)
        zrow[d, 1 + cells : 1 + 2 * cells, :] = high
        zrow[d, 1 : 1 + cells, :] = mid
        zrow[d, 0:1, :] = low[cells - 1 : cells]


def own_rows(own, cells):
    return [own[d * cells : (d + 1) * cells, :] for d in range(3)]


def first_kernel(
    sizes, counts_ref, packed, in_w, basis_w, basis_b, filt_w, filt_b, dense_w, dense_b, final_w, final_b,
    acc, w1, w2, in_t, dense_o, final_o, biases, by_j, pick, own, filled, proj, zrow, rads, wgts
):
    cells, a, f, k = sizes
    lanes, base = a * a, cells * a
    w1[...] = jnp.zeros(w1.shape, BF16)
    w1[:, :k] = (basis_w[...].astype(F32).T * LOG2_E).astype(BF16)
    bias = (basis_b[...] * LOG2_E - 1.0).T
    for n, part in enumerate(split_bf16(bias, 3)):
        w1[:, PAD_K + n : PAD_K + n + 1] = part
    w2[...] = jnp.zeros(w2.shape, BF16)
    w2[:, :f] = filt_w[...].astype(F32).T.astype(BF16)
    for n, part in enumerate(split_bf16(filt_b[...].T * LOG2_E, 2)):
        w2[:, f + n : f + n + 1] = part
    in_t[...] = in_w[...].astype(F32).T.astype(BF16)
    dense_o[...] = dense_w[...]
    final_o[...] = final_w[...]
    biases[0:1, :] = dense_b[...]
    biases[1:2, :] = final_b[...]
    slot = lax.broadcasted_iota(jnp.int32, (a, f), 0)
    for c in range(cells):
        filled[c * a : (c + 1) * a, :] = (slot < counts_ref[c]).astype(F32)
    by_j[...] = spread(a, lanes, f, True, spot_groups(cells))
    pick[...] = spread(a, lanes, a, False)
    line = packed.reshape(1, *packed.shape)
    own[...] = spots(line, 0, base, spread(a, lanes, f, False, spot_groups(cells)))
    table = spots(line, 0, base, by_j)
    window(zrow, (table, table, table), cells)
    small = lax.broadcasted_iota(jnp.int32, (1, lanes), 1)
    other = small % a != small // a
    project(proj, [(c, line, 0, c) for c in range(cells)], in_t, a)
    for r in range(3):
        there = [zrow[d, r : r + cells, :] for d in range(3)]
        moves = ((0,), (0,), (r - 1,))
        rads[r], wgts[r] = pair_terms(there, own_rows(own, cells), moves, other if r == 1 else None)
    acc[...] = jnp.zeros(acc.shape, F32)
    units = [unit(rads, wgts, proj, c, r, c + r - 1) for c, r in inside(cells)]
    add_pairs(units, cells, lanes, w1, w2, acc, k, f)


def near_kernel(sizes, line, low_line, high_line, own, w1, w2, in_t, by_j, acc0, acc, proj, zrow, rads, wgts):
    cells, a, f, k = sizes
    lanes, base, wide = a * a, cells * a, cells + 2
    slots = []
    for p in range(3):
        slots += [(p * wide, low_line, p, cells - 1), (p * wide + cells + 1, high_line, p, 0)]
        slots += [(p * wide + c + 1, line, p, c) for c in range(cells if p != 1 else 0)]
        window(zrow, [spots(l, p, base, by_j) for l in (low_line, line, high_line)], cells)
        for r in range(3):
            there = [zrow[d, r : r + cells, :] for d in range(3)]
            moves = ((1 - p,), (0,), (r - 1,))
            rads[p * 3 + r], wgts[p * 3 + r] = pair_terms(there, own_rows(own, cells), moves, None)
    project(proj, slots, in_t, a)
    units = []
    for p in range(3):
        spans = [(c, r) for c in range(cells) for r in range(3)] if p != 1 else [(0, 0), (cells - 1, 2)]
        units += [unit(rads, wgts, proj, c, p * 3 + r, p * wide + c + r) for c, r in spans]
    units.sort(key=lambda u: u[0])
    add_pairs(units, cells, lanes, w1, w2, acc, k, f, acc0)


def plane_kernel(sizes, ways, *refs):
    cells, a, f, k = sizes
    lines, refs = refs[: len(ways)], refs[len(ways) :]
    own, w1, w2, in_t, by_j, acc1, acc, proj, zrow, rads, wgts = refs
    lanes, base, n_ways = a * a, cells * a, len(ways)
    slots = []
    for p in range(3):
        for way, moves_y in enumerate(ways):
            at = p * n_ways + way
            slots += [(at * cells + c, lines[way], p, c) for c in range(cells)]
            window(zrow, [spots(lines[way], p, base, by_j)] * 3, cells)
            for r in range(3):
                there = [zrow[d, r : r + cells, :] for d in range(3)]
                moves = ((1 - p,), moves_y, (r - 1,))
                rads[at * 3 + r], wgts[at * 3 + r] = pair_terms(there, own_rows(own, cells), moves, None)
    project(proj, slots, in_t, a)
    units = []
    for at in range(3 * n_ways):
        units += [unit(rads, wgts, proj, c, at * 3 + r, at * cells + c + r - 1) for c, r in inside(cells)]
    units.sort(key=lambda u: (u[0] in (0, cells - 1), u[0]))
    add_pairs(units, cells, lanes, w1, w2, acc, k, f, acc1)


def last_kernel(sizes, ways, sides, *refs):
    cells, a, f, k = sizes
    lows, highs = refs[: len(ways)], refs[(sides - 1) * len(ways) : sides * len(ways)]
    refs = refs[sides * len(ways) :]
    packed, own, w1, w2, in_t, by_j, pick, dense_w, final_w, biases, filled, acc2 = refs[:12]
    out_ref, acc, proj, gaps, rads, wgts = refs[12:]
    lanes, base, n_ways = a * a, cells * a, len(ways)
    coords = own_rows(own, cells)
    edge = [(p, way, high) for p in range(3) for way in range(n_ways) for high in range(2)]
    count = len(edge)
    slots, units = [], []
    low_rows = [[spots(block, p, base, by_j) for p in range(3)] for block in lows]
    high_rows = low_rows
    if highs[0] is not lows[0]:
        high_rows = [[spots(block, p, base, by_j) for p in range(3)] for block in highs]
    for at, (p, way, high) in enumerate(edge):
        block, cell, c = (highs[way], 0, cells - 1) if high else (lows[way], cells - 1, 0)
        slots.append((at, block, p, cell))
        table = (high_rows if high else low_rows)[way][p]
        for d in range(3):
            row = d * cells + cell
            gaps[d, at : at + 1, :] = table[row : row + 1] - coords[d][c : c + 1]
        units.append((
            c, lambda at=at: rads[at : at + 1, :], lambda at=at: wgts[at : at + 1, :], lambda at=at: proj[at],
        ))
    project(proj, slots, in_t, a)
    index = lax.broadcasted_iota(jnp.int32, (count, lanes), 0)

    def per_row(value):
        out = jnp.zeros((count, lanes), F32)
        for at, key in enumerate(edge):
            if value(*key):
                out = jnp.where(index == at, float(value(*key)), out)
        return out

    gap = [gaps[d, 0:count, :] for d in range(3)]
    gap[0] = gap[0] + per_row(lambda p, way, high: 1 - p)
    gap[2] = gap[2] + per_row(lambda p, way, high: 2 * high - 1)
    if n_ways == 1:
        gap[1] = jnp.minimum(jnp.abs(gap[1] + 1.0), jnp.abs(gap[1] - 1.0))
    else:
        gap[1] = gap[1] + per_row(lambda p, way, high: ways[way][0])
    rads[...], wgts[...] = pair_terms(gap, None, None, None)
    units.sort(key=lambda u: u[0])
    add_pairs(units, cells, lanes, w1, w2, acc, k, f, acc2)

    messages = []
    for c in range(cells):
        head = (acc if c in (0, cells - 1) else acc2)[c].astype(BF16)
        messages.append(lax.dot_general(pick[...], head, NT, preferred_element_type=F32))
    message = jnp.concatenate(messages, axis=0).astype(BF16)
    inner = jnp.dot(message, dense_w[...], preferred_element_type=F32) + biases[0:1, :]
    inner = (jnp.maximum(inner, 0.0) + jnp.log(0.5 + 0.5 * jnp.exp(-jnp.abs(inner)))).astype(BF16)
    update = jnp.dot(inner, final_w[...], preferred_element_type=F32) + biases[1:2, :]
    value = (packed[: cells * a, :].astype(F32) + update) * filled[...]
    for c in range(cells):
        out_ref[c] = value[c * a : (c + 1) * a].astype(BF16)


def shifted(value, steps):
    axes = [axis for axis, s in steps if s % lax.axis_size(axis)]
    if not axes:
        return value
    sizes = [lax.axis_size(axis) for axis in axes]
    moves = [dict(steps)[axis] for axis in axes]
    pairs = []
    for at in np.ndindex(*sizes):
        to = [(i + s) % n for i, s, n in zip(at, moves, sizes)]
        pairs.append((int(np.ravel_multi_index(at, sizes)), int(np.ravel_multi_index(to, sizes))))
    return lax.ppermute(value, tuple(axes), pairs)


def on_chip(value):
    return pltpu.with_memory_space_constraint(value, pltpu.VMEM)


def shards(
    atoms,
    places,
    counts,
    in_weight,
    basis_weight,
    basis_bias,
    filter_weight,
    filter_bias,
    dense_weight,
    dense_bias,
    final_weight,
    final_bias,
):
    cells_x, cells_y, cells_z, a, f = atoms.shape
    assert cells_x == 1 and cells_y == 1 and a == SLOTS
    cells = cells_z
    k = basis_weight.shape[0]
    lanes = a * a
    sizes = (cells, a, f, k)
    vmem = pl.BlockSpec(memory_space=pltpu.VMEM)
    smem = pl.BlockSpec(memory_space=pltpu.SMEM)
    counts = counts.reshape(cells)
    packed = pl.pallas_call(
        pack_kernel,
        out_shape=pltpu.VMEM((cells * a + SPOT_ROWS, f), BF16),
        in_specs=[smem, vmem, vmem],
        out_specs=vmem,
    )(counts, atoms.reshape(cells, a, f), jnp.swapaxes(places, 2, 3).reshape(3, cells, a))
    above = shifted(packed, [("gx", -1)])
    below = shifted(packed, [("gx", 1)])
    sums = pltpu.VMEM((cells, f, lanes), F32)
    row = pltpu.VMEM((3, 16, lanes), F32)

    def call(kernel, out_shape, scratch, args, scalars=()):
        single = not isinstance(out_shape, list)
        return pl.pallas_call(
            kernel,
            out_shape=out_shape,
            in_specs=[smem] * len(scalars) + [vmem] * len(args),
            out_specs=vmem if single else [vmem] * len(out_shape),
            scratch_shapes=scratch,
            cost_estimate=pl.CostEstimate(flops=10**9, transcendentals=10**6, bytes_accessed=10**6),
        )(*scalars, *args)

    def tiles(n):
        return pltpu.VMEM((n, f, 128), F32)

    def terms(n, rows):
        return [pltpu.VMEM((n, rows, lanes), F32)] * 2

    acc0, w1, w2, in_t, dense_w, final_w, biases, by_j, pick, own, filled = call(
        lambda *refs: first_kernel(sizes, *refs),
        [
            sums,
            pltpu.VMEM((f, PAD_K + 8), BF16),
            pltpu.VMEM((f, f + EXTRA), BF16),
            pltpu.VMEM((f, f), BF16),
            pltpu.VMEM((f, f), BF16),
            pltpu.VMEM((f, f), BF16),
            pltpu.VMEM((2, f), F32),
            pltpu.VMEM((f, spot_groups(cells) * lanes), BF16),
            pltpu.VMEM((a, lanes), BF16),
            pltpu.VMEM((16, lanes), F32),
            pltpu.VMEM((cells * a, f), F32),
        ],
        [tiles(cells), row] + terms(3, cells),
        (
            on_chip(packed),
            in_weight,
            basis_weight,
            basis_bias.reshape(1, f),
            filter_weight,
            filter_bias.reshape(1, f),
            dense_weight,
            dense_bias.reshape(1, f),
            final_weight,
            final_bias.reshape(1, f),
        ),
        (counts,),
    )
    above, below, acc0 = lax.optimization_barrier((above, below, acc0))
    line = jnp.stack([above, packed, below])

    y_steps, ways = ([1], [(1, -1)]) if lax.axis_size("gy") == 2 else ([1, -1], [(1,), (-1,)])
    z_steps = [1] if lax.axis_size("gz") == 2 else [-1, 1]
    y_lines = [shifted(line, [("gy", -y)]) for y in y_steps]
    near_z = [shifted(line, [("gz", -z)]) for z in z_steps]

    n_ways = len(ways)
    shared = tuple(map(on_chip, (own, w1, w2, in_t, by_j)))
    acc1 = call(
        lambda *refs: near_kernel(sizes, *refs),
        sums,
        [tiles(3 * (cells + 2)), row] + terms(9, cells),
        (on_chip(line), on_chip(near_z[0]), on_chip(near_z[-1])) + shared + (on_chip(acc0),),
    )
    y_lines, acc1 = lax.optimization_barrier((y_lines, acc1))
    far_z = [[shifted(y_line, [("gz", -z)]) for z in z_steps] for y_line in y_lines]
    acc2 = call(
        lambda *refs: plane_kernel(sizes, ways, *refs),
        sums,
        [tiles(3 * n_ways * cells), row] + terms(9 * n_ways, cells),
        tuple(map(on_chip, y_lines)) + shared + (on_chip(acc1),),
    )
    far_z, acc2 = lax.optimization_barrier((far_z, acc2))
    out = call(
        lambda *refs: last_kernel(sizes, ways, len(z_steps), *refs),
        jax.ShapeDtypeStruct((cells, a, f), BF16),
        [sums, tiles(6 * n_ways), pltpu.VMEM((3, 8 * n_ways, lanes), F32)]
        + [pltpu.VMEM((6 * n_ways, lanes), F32)] * 2,
        tuple(map(on_chip, [z[side] for side in range(len(z_steps)) for z in far_z] + [packed]))
        + shared
        + tuple(map(on_chip, (pick, dense_w, final_w, biases, filled, acc2))),
    )
    return out.reshape(atoms.shape)


def solution(mesh):
    placed = (
        P(("groups", "gx"), "gy", "gz", None, None),
        P(("groups", "gx"), "gy", "gz", None, None),
        P(("groups", "gx"), "gy", "gz"),
    ) + (P(),) * 9
    return jax.shard_map(
        shards,
        mesh=mesh,
        in_specs=placed,
        out_specs=P(("groups", "gx"), "gy", "gz", None, None),
        check_vma=False,
    )
```
